128 devices in a mesh: grp: 8 (over x, core), blk: 16 (over y, z).
Axes of the slice: x: 4, y: 4, z: 4, core: 2. Of those that a mesh axis runs over, the one named last changes fastest.
Arguments:
- vector: bfloat16 [128, 512], P(('grp', 'blk')), may hold values from -6 to 6
- integrals: bfloat16 [1024, 500, 500], P(('grp', 'blk')), may hold values from -0.072 to 0.072
- orbitals: bfloat16 [26, 500], replicated, may hold values from -0.25 to 0.25
- alpha_addr: int32 [128, 676], replicated, may hold values from 0 to 127
- alpha_sign: int32 [128, 676], replicated, may hold values from -1 to 1
- beta_addr: int32 [512, 676], replicated, may hold values from 0 to 511
- beta_sign: int32 [512, 676], replicated, may hold values from -1 to 1
- seg_alpha: int32 [128], replicated, may hold values from 0 to 9, never falling along the last dimension, each value on 1 to 25 neighbouring positions
- seg_beta: int32 [512], replicated, may hold values from 0 to 9, never falling along the last dimension, each value on 1 to 102 neighbouring positions
- allowed: int32 [10, 10], replicated, may hold values 0 or 1
Outputs:
- sigma_t: float32 [512, 128], P(('grp', 'blk'))
The draws below stay inside these ranges and needn't reach their ends.
All inputs are finite; a program needn't handle non-finite values.
Results may differ from the reference program's by a relative error of at most 0.0056.
Values may be sent and summed in bfloat16 or wider, within the bound.
A program may use at most 64 MiB of HBM per device.

```python
import math
import jax
import jax.numpy as jnp
import numpy as np
from jax import lax

NORB = 26
NPAIR = 676
NBAS = 500
NAUX = 1024
NBLK = 10
B_DEV = 4
NA = 128
NB = 512


def draw_integrals(key, part):
    levels = jnp.arange(NAUX, dtype=jnp.float32) / NAUX
    scales = (0.003 * jnp.power(4.0, levels))[:, None, None]
    values = jnp.clip(jax.random.normal(key, (NAUX, NBAS, NBAS), jnp.float32), -6.0, 6.0)
    return (values * scales).astype(jnp.bfloat16)


def with_ends(values, key, low, high):
    place = [jax.random.randint(jax.random.fold_in(key, axis), (), 0, length) for axis, length in enumerate(values.shape)]
    main_axis = values.shape.index(max(values.shape))
    next_to = place[:main_axis] + [(place[main_axis] + 1) % values.shape[main_axis]] + place[main_axis + 1:]
    return values.at[tuple(place)].set(low).at[tuple(next_to)].set(high)


def shard_levels(rng, extent, split, least, high):
    loudness = 1.0
    for position, shards_of in split:
        heights = jax.random.uniform(jax.random.fold_in(jax.random.fold_in(rng, 6), position), (shards_of,), jnp.float32, least / len(split), high / len(split))
        loudness = loudness * jnp.repeat(jnp.exp(heights), extent[position] // shards_of).reshape((-1,) + (1,) * (len(extent) - 1 - position))
    return loudness


def split_up(amount, total, bound, skew):
    weights = [(1 << 20) // math.isqrt(standing ** skew) + 1 for standing in range(2, amount + 1)]
    surplus, given = total - bound - (amount - 1), [1] * (amount - 1)
    while surplus > 0:
        candidates = [i for i in range(amount - 1) if given[i] < bound]
        pool, budget = sum([weights[i] for i in candidates]), surplus
        for i in candidates:
            more = min(bound - given[i], max(1, budget * weights[i] // pool), surplus)
            given[i] = given[i] + more
            surplus = surplus - more
    return np.array([bound] + given)


def ragged(key, count, total, limit, lean):
    if count == 2:
        one = jax.random.randint(key, (), max(1, total - limit), min(limit, total - 1) + 1)
        return jnp.stack([one, total - one])
    lengths = jnp.asarray(split_up(count, total, limit, lean), jnp.int32)
    pairs = (count - 1) // 2
    giver, receiver = lengths[1:1 + 2 * pairs:2], lengths[2:2 + 2 * pairs:2]
    margin = jnp.minimum(giver - 1, limit - receiver)
    moved = jax.random.randint(jax.random.fold_in(key, 1), (pairs,), 0, 1 << 20) % (margin + 1)
    lengths = lengths.at[1:1 + 2 * pairs:2].set(giver - moved).at[2:2 + 2 * pairs:2].set(receiver + moved)
    return lengths[jax.random.permutation(jax.random.fold_in(key, 2), count)]


def normal_values(stream_key, shape, scale, reach, shards=(), kind=jnp.bfloat16):
    entries = jax.random.normal(stream_key, shape, jnp.float32) * scale
    if len(shards) > 0:
        entries = shard_levels(stream_key, shape, shards, -0.22, 0.18) * entries
    return jnp.clip(entries, min=-reach, max=reach).astype(kind)


def setup_inputs(seed: int = 0) -> dict:
    key_list = jax.random.split(jax.random.key(seed), 11)
    vector = normal_values(key_list[0], (NA, NB), 1.0, 6.0, ((0, 128),))
    integrals = draw_integrals(jax.random.fold_in(key_list[10], 71), 0)
    orbitals = normal_values(key_list[2], (NORB, NBAS), NBAS ** -0.5, 0.25)
    alpha_addr = with_ends(jax.random.randint(key_list[3], (NA, NPAIR), 0, NA), jax.random.fold_in(key_list[3], 1), 0, NA - 1).astype(jnp.int32)
    alpha_sign = with_ends(jax.random.randint(key_list[4], (NA, NPAIR), -1, 2), jax.random.fold_in(key_list[4], 1), -1, 1).astype(jnp.int32)
    beta_addr = with_ends(jax.random.randint(key_list[5], (NB, NPAIR), 0, NB), jax.random.fold_in(key_list[5], 1), 0, NB - 1).astype(jnp.int32)
    beta_sign = with_ends(jax.random.randint(key_list[6], (NB, NPAIR), -1, 2), jax.random.fold_in(key_list[6], 1), -1, 1).astype(jnp.int32)
    seg_alpha = jnp.searchsorted(jnp.cumsum(ragged(key_list[7], NBLK, NA, 2 * NA // NBLK, 2)), jnp.arange(NA), side="right").astype(jnp.int32)
    seg_beta = jnp.searchsorted(jnp.cumsum(ragged(key_list[8], NBLK, NB, 2 * NB // NBLK, 2)), jnp.arange(NB), side="right").astype(jnp.int32)
    allowed = with_ends((jax.random.randint(key_list[9], (NBLK, NBLK), 0, 4) < 3).astype(jnp.int32), jax.random.fold_in(key_list[9], 1), 0, 1)
    return dict(vector=vector, integrals=integrals, orbitals=orbitals, alpha_addr=alpha_addr, alpha_sign=alpha_sign, beta_addr=beta_addr, beta_sign=beta_sign, seg_alpha=seg_alpha, seg_beta=seg_beta, allowed=allowed)


def onehot(segment_ids):
    return (segment_ids[:, None] == jnp.arange(NBLK, dtype=jnp.int32)[None, :]).astype(jnp.float32)


def reference(vector, integrals, orbitals, alpha_addr, alpha_sign, beta_addr, beta_sign, seg_alpha, seg_beta, allowed):
    allowed_f = allowed.astype(jnp.float32)
    det_mask = jnp.dot(jnp.dot(onehot(seg_alpha), allowed_f, precision=lax.Precision.HIGHEST), onehot(seg_beta).T, precision=lax.Precision.HIGHEST)
    masked = (vector.astype(jnp.float32) * det_mask).astype(jnp.bfloat16)
    orbital_f = orbitals.astype(jnp.float32)

    def transform(slab):
        half_done = jnp.einsum('jn,pmn->pjm', orbital_f, slab.astype(jnp.float32)).astype(jnp.bfloat16)
        return jnp.einsum('im,pjm->pij', orbital_f, half_done.astype(jnp.float32)).astype(jnp.bfloat16)

    factors = lax.map(transform, integrals.reshape(-1, 8, NBAS, NBAS)).reshape(NAUX, NPAIR)
    factor_f = factors.astype(jnp.float32)
    coulomb = jnp.dot(factor_f.T, factor_f, precision=lax.Precision.HIGHEST).astype(jnp.bfloat16)
    coulomb_f = coulomb.astype(jnp.float32)
    beta_local = jnp.arange(B_DEV, dtype=jnp.int32)
    pair_ids = jnp.arange(NPAIR, dtype=jnp.int32)
    sign_alpha = alpha_sign.astype(jnp.float32)

    def beta_block(tables):
        block_addr, block_sign = tables
        pair_terms = jnp.take(masked, block_addr, axis=1) * block_sign.astype(jnp.bfloat16)[None]
        products = jnp.dot(pair_terms.reshape(-1, NPAIR).astype(jnp.float32), coulomb_f.T, precision=lax.Precision.HIGHEST)
        flattened = products.astype(jnp.bfloat16).reshape(-1)
        gather_index = alpha_addr[None, :, :] * (B_DEV * NPAIR) + beta_local[:, None, None] * NPAIR + pair_ids[None, None, :]
        picked = jnp.take(flattened, gather_index).astype(jnp.float32)
        return jnp.sum(picked * sign_alpha[None], axis=2)

    sigma_all = lax.map(beta_block, (beta_addr.reshape(-1, B_DEV, NPAIR), beta_sign.reshape(-1, B_DEV, NPAIR)))
    return sigma_all.reshape(NB, NA) * det_mask.T
```

```python
import jax
import jax.numpy as jnp
from jax import lax
from jax.experimental import pallas as pl
from jax.experimental.pallas import tpu as pltpu
from jax.sharding import PartitionSpec as P

MESH = pl.DeviceIdType.MESH
SIDE = 4
LANES = 128
NORB = 26
ROWS = 32
NPAIR = NORB * NORB
WIDE = 768
TALL = 680
PART = 256
ORDERS = ((2, 1, 0), (0, 2, 1), (1, 0, 2))
NBLK = 10


def kernel(
    vec_hbm, int_hbm, orb_hbm, aaddr_hbm, asign_hbm, baddr_hbm, bsign_hbm, sega_hbm, segb_hbm, allow_hbm,
    out_ref,
    vec_v, ibuf, orb_v, orb32, orbe, hbuf, araw, sraw, atab, stab, btab, bsgn, sega_v, segb_v, sega_s, segb_s, allow_s,
    fbuf, vbuf, vf32, mbuf, ptt, fmat, fmat_t, tmat, pmat, sig_out, sig_in,
    isem, lsem, f_send, f_recv, v_send, v_recv, s_send, s_recv, c_send, c_recv,
):
    grp = lax.axis_index("grp")
    blk = lax.axis_index("blk")
    core = lax.rem(grp, 2)
    here = (lax.div(grp, 2), lax.div(blk, SIDE), lax.rem(blk, SIDE))
    x, y, z = here
    position = grp * (SIDE * SIDE) + blk
    n_aux = int_hbm.shape[0]
    n_alpha = aaddr_hbm.shape[0]

    def device_at(axis, step):
        spot = list(here)
        spot[axis] = lax.rem(spot[axis] + step, SIDE)
        return (spot[0] * 2 + core, spot[1] * SIDE + spot[2])

    sibling = (x * 2 + (1 - core), blk)

    eight = pl.multiple_of(lax.div(position, 2) * 8, 8)
    twin_position = (x * 2 + (1 - core)) * (SIDE * SIDE) + blk
    twin_eight = pl.multiple_of(lax.div(twin_position, 2) * 8, 8)
    local = [
        (vec_hbm, vec_v),
        (segb_hbm, segb_v),
        (sega_hbm, sega_s),
        (allow_hbm, allow_s),
        (orb_hbm, orb_v),
        (sega_hbm, sega_v),
        (segb_hbm, segb_s),
        (baddr_hbm.at[pl.ds(twin_eight, 8), :], btab.at[pl.ds(0, 8), :]),
        (baddr_hbm.at[pl.ds(eight, 8), :], btab.at[pl.ds(8, 8), :]),
        (bsign_hbm.at[pl.ds(twin_eight, 8), :], bsgn.at[pl.ds(0, 8), :]),
        (bsign_hbm.at[pl.ds(eight, 8), :], bsgn.at[pl.ds(8, 8), :]),
        (aaddr_hbm, araw),
        (asign_hbm, sraw),
    ]
    local = [pltpu.make_async_copy(src, dst, lsem.at[i]) for i, (src, dst) in enumerate(local)]
    slabs = [pltpu.make_async_copy(int_hbm.at[p], ibuf.at[p], isem.at[p]) for p in range(n_aux)]
    for copy in local[:5]:
        copy.start()
    for copy in slabs:
        copy.start()
    for copy in local[5:]:
        copy.start()

    barrier = pltpu.get_barrier_semaphore()
    for axis in range(3):
        for step in range(1, SIDE):
            pl.semaphore_signal(barrier, inc=1, device_id=device_at(axis, step), device_id_type=MESH)
    pl.semaphore_signal(barrier, inc=1, device_id=sibling, device_id_type=MESH)

    for copy in local[:4]:
        copy.wait()
    seg_here = sega_s[0, position]
    row_mask = jnp.zeros(segb_v.shape, jnp.float32)
    for block in range(NBLK):
        row_mask = jnp.where(segb_v[...] == block, allow_s[seg_here, block].astype(jnp.float32), row_mask)
    masked = vec_v[...].astype(jnp.float32) * row_mask
    pieces = [masked[:, i * LANES : (i + 1) * LANES] for i in range(4)] + [jnp.zeros((4, LANES), jnp.float32)]
    vbuf[x, core, y, z] = jnp.concatenate(pieces, axis=0).astype(jnp.bfloat16)

    def v_copy(stage, step):
        place = (
            vbuf.at[x, core, y, z],
            vbuf.at[x, core, y],
            vbuf.at[x, core],
        )[stage]
        return pltpu.make_async_remote_copy(
            src_ref=place, dst_ref=place,
            send_sem=v_send.at[stage, step - 1], recv_sem=v_recv.at[stage, step - 1],
            device_id=device_at(2 - stage, step), device_id_type=MESH,
        )

    def f_copy(part, stage, step):
        order = ORDERS[part]
        index = tuple(slice(None) if axis in order[:stage] else here[axis] for axis in range(3))
        place = fbuf.at[index + (slice(None), pl.ds(part * PART, PART))]
        return pltpu.make_async_remote_copy(
            src_ref=place, dst_ref=place,
            send_sem=f_send.at[part, stage, step - 1], recv_sem=f_recv.at[part, stage, step - 1],
            device_id=device_at(order[stage], step), device_id_type=MESH,
        )

    v_twin = pltpu.make_async_remote_copy(
        src_ref=vbuf.at[:, core], dst_ref=vbuf.at[:, core], send_sem=c_send, recv_sem=c_recv,
        device_id=sibling, device_id_type=MESH,
    )

    def v_start(stage):
        for step in range(1, SIDE):
            v_copy(stage, step).start()

    def v_wait(stage):
        for step in range(1, SIDE):
            v_copy(stage, step).wait_recv()

    def f_start(stage):
        for part in range(3):
            for step in range(1, SIDE):
                f_copy(part, stage, step).start()

    pl.semaphore_wait(barrier, 10)
    v_start(0)

    local[4].wait()
    orb32[...] = jnp.zeros_like(orb32)
    orb32[0:NORB, :] = orb_v[...]
    lane = lax.broadcasted_iota(jnp.int32, (1, WIDE), 1)
    first = jnp.zeros((1, WIDE), jnp.int32)
    for i in range(1, NORB + 1):
        first = first + jnp.where(lane >= i * NORB, 1, 0)
    second = lane - NORB * first
    row = lax.broadcasted_iota(jnp.int32, (ROWS, WIDE), 0)
    spread = jnp.where(row == first, 1.0, 0.0).astype(jnp.bfloat16)
    orbe[...] = lax.dot_general(
        orb32[...], spread, (((0,), (0,)), ((), ())), preferred_element_type=jnp.float32
    ).astype(jnp.bfloat16)

    for p in range(n_aux):
        slabs[p].wait()
        hbuf[p * ROWS : (p + 1) * ROWS, :] = lax.dot_general(
            orb32[...], ibuf[p], (((1,), (1,)), ((), ())), preferred_element_type=jnp.float32
        ).astype(jnp.bfloat16)
    whole = jnp.dot(hbuf[...], orbe[...], preferred_element_type=jnp.float32)
    whole = jnp.where((row == second)[None], whole.reshape(n_aux, ROWS, WIDE), 0.0)
    fbuf[x, y, z] = jnp.sum(whole, axis=1).astype(jnp.bfloat16)
    f_start(0)

    v_wait(0)
    v_start(1)

    def f_pass(stage):
        for part in range(3):
            for step in range(1, SIDE):
                f_copy(part, stage, step).wait_recv()
            if stage < 2:
                for step in range(1, SIDE):
                    f_copy(part, stage + 1, step).start()

    f_pass(0)
    v_wait(1)
    v_start(2)
    f_pass(1)
    v_wait(2)
    v_twin.start()

    local[11].wait()
    local[12].wait()
    atab[TALL - 8 : TALL, :] = jnp.zeros((8, n_alpha), jnp.int32)
    stab[TALL - 8 : TALL, :] = jnp.zeros((8, n_alpha), jnp.float32)
    atab[0:NPAIR, :] = araw[...].T
    stab[0:NPAIR, :] = sraw[...].astype(jnp.float32).T

    for copy in local[7:11]:
        copy.wait()
    v_twin.wait_recv()
    vf32[...] = vbuf[...].astype(jnp.float32).reshape(n_alpha * 8, LANES)
    for i in range(4):
        mbuf[:, i * LANES : (i + 1) * LANES] = vf32[pl.ds(i, n_alpha, stride=8), :].astype(jnp.bfloat16)

    n_beta = mbuf.shape[1]
    offset = lax.rem(position, 2) * 4

    @pl.loop(0, 8)
    def _(i):
        where = lax.div(i, 4) * 8 + offset + lax.rem(i, 4)
        addr = btab[pl.ds(where, 1), :]
        sign = bsgn[pl.ds(where, 1), :].astype(jnp.float32)
        beta = lax.broadcasted_iota(jnp.int32, (n_beta, NPAIR), 0)
        table = jnp.where(beta == addr, sign, 0.0).astype(jnp.bfloat16)
        ptt[pl.ds(pl.multiple_of(i * n_alpha, n_alpha), n_alpha), :] = jnp.dot(
            mbuf[...], table, preferred_element_type=jnp.float32
        ).astype(jnp.bfloat16)

    f_pass(2)
    count = fmat.shape[0]
    fmat[...] = fbuf[...].astype(jnp.float32).reshape(count, WIDE).astype(jnp.bfloat16)
    fmat_t[...] = fmat[...].T

    def half_sigma(half):
        rows = 4 * n_alpha
        tmat[...] = lax.dot_general(
            fmat[:, 0:NPAIR], ptt[half * rows : (half + 1) * rows, :],
            (((1,), (1,)), ((), ())), preferred_element_type=jnp.float32,
        ).astype(jnp.bfloat16)
        pmat[...] = jnp.dot(fmat_t[0:TALL, :], tmat[...], preferred_element_type=jnp.float32)

        def add_rows(i, totals):
            at = pl.ds(pl.multiple_of(i * 8, 8), 8)
            index = atab[at, :]
            sign = stab[at, :]
            return tuple(
                total + sign * jnp.take_along_axis(
                    pmat[at, b * n_alpha : (b + 1) * n_alpha], index, axis=1, mode="promise_in_bounds"
                )
                for b, total in enumerate(totals)
            )

        totals = lax.fori_loop(0, TALL // 8, add_rows, (jnp.zeros((8, n_alpha), jnp.float32),) * 4)
        return jnp.concatenate([jnp.sum(total, axis=0, keepdims=True) for total in totals], axis=0)

    sig_out[0:4, :] = half_sigma(0)
    s_copy = pltpu.make_async_remote_copy(
        src_ref=sig_out, dst_ref=sig_in, send_sem=s_send, recv_sem=s_recv,
        device_id=sibling, device_id_type=MESH,
    )
    s_copy.start()
    mine = half_sigma(1)
    local[5].wait()
    local[6].wait()
    column = []
    for b in range(4):
        seg = segb_s[0, position * 4 + b]
        mask = jnp.zeros((1, n_alpha), jnp.float32)
        for block in range(NBLK):
            mask = jnp.where(sega_v[...] == block, allow_s[block, seg].astype(jnp.float32), mask)
        column.append(mask)
    s_copy.wait_recv()
    out_ref[...] = (mine + sig_in[0:4, :]) * jnp.concatenate(column, axis=0)

    for stage in range(3):
        for step in range(1, SIDE):
            v_copy(stage, step).wait_send()
            for part in range(3):
                f_copy(part, stage, step).wait_send()
    v_twin.wait_send()
    s_copy.wait_send()


def on_device(
    vector, integrals, orbitals, alpha_addr, alpha_sign, beta_addr, beta_sign, seg_alpha, seg_beta, allowed
):
    n_aux, n_bas, _ = integrals.shape
    n_alpha = alpha_addr.shape[0]
    n_beta = beta_addr.shape[0]
    bf16, f32, i32 = jnp.bfloat16, jnp.float32, jnp.int32
    vmem, smem, dma = pltpu.VMEM, pltpu.SMEM, pltpu.SemaphoreType.DMA
    chips = SIDE**3
    return pl.pallas_call(
        kernel,
        out_shape=jax.ShapeDtypeStruct((n_beta // (2 * chips), n_alpha), f32),
        in_specs=[pl.BlockSpec(memory_space=pl.ANY)] * 10,
        out_specs=pl.BlockSpec(memory_space=pltpu.VMEM),
        scratch_shapes=[
            vmem((1, n_beta), bf16),
            vmem((n_aux, n_bas, n_bas), bf16),
            vmem((NORB, n_bas), bf16),
            vmem((ROWS, n_bas), bf16),
            vmem((n_bas, WIDE), bf16),
            vmem((n_aux * ROWS, n_bas), bf16),
            vmem((n_alpha, NPAIR), i32),
            vmem((n_alpha, NPAIR), i32),
            vmem((TALL, n_alpha), i32),
            vmem((TALL, n_alpha), f32),
            vmem((16, NPAIR), i32),
            vmem((16, NPAIR), i32),
            vmem((1, n_alpha), i32),
            vmem((1, n_beta), i32),
            smem((1, n_alpha), i32),
            smem((1, n_beta), i32),
            smem((NBLK, NBLK), i32),
            vmem((SIDE, SIDE, SIDE, n_aux, WIDE), bf16),
            vmem((SIDE, 2, SIDE, SIDE, 8, LANES), bf16),
            vmem((n_alpha * 8, LANES), f32),
            vmem((n_alpha, n_beta), bf16),
            vmem((8 * n_alpha, NPAIR), bf16),
            vmem((chips * n_aux, WIDE), bf16),
            vmem((WIDE, chips * n_aux), bf16),
            vmem((chips * n_aux, 4 * n_alpha), bf16),
            vmem((TALL, 4 * n_alpha), f32),
            vmem((8, n_alpha), f32),
            vmem((8, n_alpha), f32),
            dma((n_aux,)),
            dma((13,)),
            dma((3, 3, SIDE - 1)),
            dma((3, 3, SIDE - 1)),
            dma((3, SIDE - 1)),
            dma((3, SIDE - 1)),
            dma,
            dma,
            dma,
            dma,
        ],
        compiler_params=pltpu.CompilerParams(
            collective_id=0, has_side_effects=True, vmem_limit_bytes=48 << 20
        ),
        name="sigma",
    )(
        vector, integrals, orbitals, alpha_addr, alpha_sign, beta_addr, beta_sign,
        seg_alpha.reshape(1, -1), seg_beta.reshape(1, -1), allowed,
    )


def solution(mesh):
    rows = P(("grp", "blk"), None)
    placed = (rows, P(("grp", "blk"), None, None)) + (P(),) * 8
    return jax.shard_map(on_device, mesh=mesh, in_specs=placed, out_specs=rows, check_vma=False)
```

```python
import jax
import jax.numpy as jnp
from jax import lax
from jax.experimental import pallas as pl
from jax.experimental.pallas import tpu as pltpu
from jax.sharding import PartitionSpec as P

MESH = pl.DeviceIdType.MESH
SIDE = 4
LANES = 128
NORB = 26
ROWS = 32
NPAIR = NORB * NORB
WIDE = 768
TALL = 680
PART = 256
ORDERS = ((2, 1, 0), (0, 2, 1), (1, 0, 2))
NBLK = 10
CHUNK = 512


def kernel(
    vec_hbm, int_hbm, orb_hbm, aaddr_hbm, asign_hbm, baddr_hbm, bsign_hbm, sega_hbm, segb_hbm, allow_hbm,
    out_ref,
    vec_v, ibuf, orb_v, orb32, orep, wtab, araw, sraw, atab, stab, btab, bsgn, baddr_v, bsign_v,
    sega_v, segb_v, sega_s, segb_s, allow_s,
    fbuf, vbuf, vf32, mbuf, ptt, fmat, fmat_t, tmat, pmat, sig_out, sig_in,
    isem, lsem, f_send, f_recv, v_send, v_recv, s_send, s_recv, c_send, c_recv,
):
    grp = lax.axis_index("grp")
    blk = lax.axis_index("blk")
    core = lax.rem(grp, 2)
    here = (lax.div(grp, 2), lax.div(blk, SIDE), lax.rem(blk, SIDE))
    x, y, z = here
    position = grp * (SIDE * SIDE) + blk
    n_aux = fbuf.shape[3]
    n_alpha = aaddr_hbm.shape[1]
    tall = int_hbm.shape[0]

    def device_at(axis, step):
        spot = list(here)
        spot[axis] = lax.rem(spot[axis] + step, SIDE)
        return (spot[0] * 2 + core, spot[1] * SIDE + spot[2])

    sibling = (x * 2 + (1 - core), blk)

    local = [
        (vec_hbm, vec_v),
        (segb_hbm, segb_v),
        (sega_hbm, sega_s),
        (allow_hbm, allow_s),
        (orb_hbm, orb_v),
        (sega_hbm, sega_v),
        (segb_hbm, segb_s),
        (baddr_hbm.at[:, pl.ds(pl.multiple_of(x * LANES, LANES), LANES)], btab),
        (bsign_hbm.at[:, pl.ds(pl.multiple_of(x * LANES, LANES), LANES)], bsgn),
        (aaddr_hbm, araw),
        (asign_hbm, sraw),
    ]
    local = [pltpu.make_async_copy(src, dst, lsem.at[i]) for i, (src, dst) in enumerate(local)]
    chunks = [(at, min(CHUNK, tall - at)) for at in range(0, tall, CHUNK)]
    slabs = [
        pltpu.make_async_copy(int_hbm.at[pl.ds(at, size), :], ibuf.at[pl.ds(at, size), :], isem.at[i])
        for i, (at, size) in enumerate(chunks)
    ]
    for copy in local[:5]:
        copy.start()
    for copy in slabs:
        copy.start()
    for copy in local[5:]:
        copy.start()

    barrier = pltpu.get_barrier_semaphore()
    for axis in range(3):
        for step in range(1, SIDE):
            pl.semaphore_signal(barrier, inc=1, device_id=device_at(axis, step), device_id_type=MESH)
    pl.semaphore_signal(barrier, inc=1, device_id=sibling, device_id_type=MESH)

    for copy in local[:4]:
        copy.wait()
    seg_here = sega_s[0, position]
    row_mask = jnp.zeros(segb_v.shape, jnp.float32)
    for block in range(NBLK):
        row_mask = jnp.where(segb_v[...] == block, allow_s[seg_here, block].astype(jnp.float32), row_mask)
    masked = vec_v[...].astype(jnp.float32) * row_mask
    pieces = [masked[:, i * LANES : (i + 1) * LANES] for i in range(4)] + [jnp.zeros((4, LANES), jnp.float32)]
    vbuf[x, core, y, z] = jnp.concatenate(pieces, axis=0).astype(jnp.bfloat16)

    def v_copy(stage, step):
        place = (
            vbuf.at[x, core, y, z],
            vbuf.at[x, core, y],
            vbuf.at[x, core],
        )[stage]
        return pltpu.make_async_remote_copy(
            src_ref=place, dst_ref=place,
            send_sem=v_send.at[stage, step - 1], recv_sem=v_recv.at[stage, step - 1],
            device_id=device_at(2 - stage, step), device_id_type=MESH,
        )

    def f_copy(part, stage, step):
        order = ORDERS[part]
        index = tuple(slice(None) if axis in order[:stage] else here[axis] for axis in range(3))
        place = fbuf.at[index + (slice(None), pl.ds(part * PART, PART))]
        return pltpu.make_async_remote_copy(
            src_ref=place, dst_ref=place,
            send_sem=f_send.at[part, stage, step - 1], recv_sem=f_recv.at[part, stage, step - 1],
            device_id=device_at(order[stage], step), device_id_type=MESH,
        )

    v_twin = pltpu.make_async_remote_copy(
        src_ref=vbuf.at[:, core], dst_ref=vbuf.at[:, core], send_sem=c_send, recv_sem=c_recv,
        device_id=sibling, device_id_type=MESH,
    )

    def v_start(stage):
        for step in range(1, SIDE):
            v_copy(stage, step).start()

    def v_wait(stage):
        for step in range(1, SIDE):
            v_copy(stage, step).wait_recv()

    def f_start(stage):
        for part in range(3):
            for step in range(1, SIDE):
                f_copy(part, stage, step).start()

    pl.semaphore_wait(barrier, 10)
    v_start(0)

    local[4].wait()
    orb32[...] = jnp.zeros_like(orb32)
    orb32[0:NORB, :] = orb_v[...]
    lane = lax.broadcasted_iota(jnp.int32, (1, WIDE), 1)
    first = jnp.zeros((1, WIDE), jnp.int32)
    for i in range(1, NORB + 1):
        first = first + jnp.where(lane >= i * NORB, 1, 0)
    second = lane - NORB * first
    row = lax.broadcasted_iota(jnp.int32, (ROWS, WIDE), 0)
    spread = jnp.where(row == second, 1.0, 0.0).astype(jnp.bfloat16)
    repeat = jnp.where(
        lax.broadcasted_iota(jnp.int32, (ROWS, n_aux * ROWS), 0)
        == lax.rem(lax.broadcasted_iota(jnp.int32, (ROWS, n_aux * ROWS), 1), ROWS),
        1.0, 0.0,
    ).astype(jnp.bfloat16)
    orep[...] = lax.dot_general(
        orb32[...], repeat, (((0,), (0,)), ((), ())), preferred_element_type=jnp.float32
    )
    same = lax.broadcasted_iota(jnp.int32, (n_aux, n_aux * ROWS), 0) == lax.div(
        lax.broadcasted_iota(jnp.int32, (n_aux, n_aux * ROWS), 1), ROWS
    )

    @pl.loop(0, tall // (n_aux * 4))
    def _(i):
        rows = [
            jnp.where(same, orep[pl.ds(i * 4 + k, 1), :], 0.0) for k in range(4)
        ]
        at = pl.multiple_of(i * (n_aux * 4), n_aux * 4)
        wtab[pl.ds(at, n_aux * 4), :] = jnp.concatenate(rows, axis=0).astype(jnp.bfloat16)

    total = jnp.zeros((ROWS, n_aux * ROWS), jnp.float32)
    for copy, (at, size) in zip(slabs, chunks):
        copy.wait()
        half = lax.dot_general(
            orb32[...], ibuf[at : at + size, :], (((1,), (1,)), ((), ())), preferred_element_type=jnp.float32
        ).astype(jnp.bfloat16)
        total = total + jnp.dot(half, wtab[at : at + size, :], preferred_element_type=jnp.float32)
    whole = lax.dot_general(
        total.astype(jnp.bfloat16), spread, (((0,), (0,)), ((), ())), preferred_element_type=jnp.float32
    )
    whole = jnp.where((row == first)[None], whole.reshape(n_aux, ROWS, WIDE), 0.0)
    fbuf[x, y, z] = jnp.sum(whole, axis=1).astype(jnp.bfloat16)
    f_start(0)

    v_wait(0)
    v_start(1)

    def f_pass(stage):
        for part in range(3):
            for step in range(1, SIDE):
                f_copy(part, stage, step).wait_recv()
            if stage < 2:
                for step in range(1, SIDE):
                    f_copy(part, stage + 1, step).start()

    f_pass(0)
    v_wait(1)
    v_start(2)
    f_pass(1)
    v_wait(2)
    v_twin.start()

    local[9].wait()
    local[10].wait()
    atab[TALL - 8 : TALL, :] = jnp.zeros((8, n_alpha), jnp.int32)
    stab[TALL - 8 : TALL, :] = jnp.zeros((8, n_alpha), jnp.float32)
    atab[0:NPAIR, :] = araw[...]
    stab[0:NPAIR, :] = sraw[...].astype(jnp.float32)

    local[7].wait()
    local[8].wait()
    string = lax.broadcasted_iota(jnp.int32, (8, LANES), 0)
    twin = jnp.where(string < 4, 1 - core, core)
    wanted = twin * (4 * SIDE * SIDE) + blk * 4 + lax.rem(string, 4)
    pick = jnp.where(lax.broadcasted_iota(jnp.int32, (8, LANES), 1) == wanted, 1.0, 0.0).astype(jnp.bfloat16)

    def picked(table):
        return lax.dot_general(
            pick, table.astype(jnp.float32).astype(jnp.bfloat16),
            (((1,), (1,)), ((), ())), preferred_element_type=jnp.float32,
        )

    addr = btab[...]
    high = lax.shift_right_logical(addr, 8)
    baddr_v[...] = (picked(addr - high * 256) + 256.0 * picked(high)).astype(jnp.int32)
    bsign_v[...] = picked(bsgn[...])
    v_twin.wait_recv()
    vf32[...] = vbuf[...].astype(jnp.float32).reshape(n_alpha * 8, LANES)
    for i in range(4):
        mbuf[:, i * LANES : (i + 1) * LANES] = vf32[pl.ds(i, n_alpha, stride=8), :].astype(jnp.bfloat16)

    n_beta = mbuf.shape[1]

    @pl.loop(0, 8)
    def _(i):
        addr = baddr_v[pl.ds(i, 1), :]
        sign = bsign_v[pl.ds(i, 1), :]
        beta = lax.broadcasted_iota(jnp.int32, (n_beta, NPAIR), 0)
        table = jnp.where(beta == addr, sign, 0.0).astype(jnp.bfloat16)
        ptt[pl.ds(pl.multiple_of(i * n_alpha, n_alpha), n_alpha), :] = jnp.dot(
            mbuf[...], table, preferred_element_type=jnp.float32
        ).astype(jnp.bfloat16)

    f_pass(2)
    count = fmat.shape[0]
    fmat[...] = fbuf[...].astype(jnp.float32).reshape(count, WIDE).astype(jnp.bfloat16)
    fmat_t[...] = fmat[...].T

    def half_sigma(half):
        rows = 4 * n_alpha
        tmat[...] = lax.dot_general(
            fmat[:, 0:NPAIR], ptt[half * rows : (half + 1) * rows, :],
            (((1,), (1,)), ((), ())), preferred_element_type=jnp.float32,
        ).astype(jnp.bfloat16)
        pmat[...] = jnp.dot(fmat_t[0:TALL, :], tmat[...], preferred_element_type=jnp.float32)

        def add_rows(i, totals):
            at = pl.ds(pl.multiple_of(i * 8, 8), 8)
            index = atab[at, :]
            sign = stab[at, :]
            return tuple(
                total + sign * jnp.take_along_axis(
                    pmat[at, b * n_alpha : (b + 1) * n_alpha], index, axis=1, mode="promise_in_bounds"
                )
                for b, total in enumerate(totals)
            )

        totals = lax.fori_loop(0, TALL // 8, add_rows, (jnp.zeros((8, n_alpha), jnp.float32),) * 4)
        return jnp.concatenate([jnp.sum(total, axis=0, keepdims=True) for total in totals], axis=0)

    sig_out[0:4, :] = half_sigma(0)
    s_copy = pltpu.make_async_remote_copy(
        src_ref=sig_out, dst_ref=sig_in, send_sem=s_send, recv_sem=s_recv,
        device_id=sibling, device_id_type=MESH,
    )
    s_copy.start()
    mine = half_sigma(1)
    local[5].wait()
    local[6].wait()
    column = []
    for b in range(4):
        seg = segb_s[0, position * 4 + b]
        mask = jnp.zeros((1, n_alpha), jnp.float32)
        for block in range(NBLK):
            mask = jnp.where(sega_v[...] == block, allow_s[block, seg].astype(jnp.float32), mask)
        column.append(mask)
    s_copy.wait_recv()
    out_ref[...] = (mine + sig_in[0:4, :]) * jnp.concatenate(column, axis=0)

    for stage in range(3):
        for step in range(1, SIDE):
            v_copy(stage, step).wait_send()
            for part in range(3):
                f_copy(part, stage, step).wait_send()
    v_twin.wait_send()
    s_copy.wait_send()


def on_device(
    vector, integrals, orbitals, alpha_addr, alpha_sign, beta_addr, beta_sign, seg_alpha, seg_beta, allowed
):
    n_aux, n_bas, _ = integrals.shape
    n_alpha = alpha_addr.shape[0]
    tall = n_aux * n_bas
    n_beta = beta_addr.shape[0]
    bf16, f32, i32 = jnp.bfloat16, jnp.float32, jnp.int32
    vmem, smem, dma = pltpu.VMEM, pltpu.SMEM, pltpu.SemaphoreType.DMA
    chips = SIDE**3
    return pl.pallas_call(
        kernel,
        out_shape=jax.ShapeDtypeStruct((n_beta // (2 * chips), n_alpha), f32),
        in_specs=[pl.BlockSpec(memory_space=pltpu.HBM)] * 10,
        out_specs=pl.BlockSpec(memory_space=pltpu.VMEM),
        scratch_shapes=[
            vmem((1, n_beta), bf16),
            vmem((tall, n_bas), bf16),
            vmem((NORB, n_bas), bf16),
            vmem((ROWS, n_bas), bf16),
            vmem((n_bas, n_aux * ROWS), f32),
            vmem((tall, n_aux * ROWS), bf16),
            vmem((NPAIR, n_alpha), i32),
            vmem((NPAIR, n_alpha), i32),
            vmem((TALL, n_alpha), i32),
            vmem((TALL, n_alpha), f32),
            vmem((NPAIR, LANES), i32),
            vmem((NPAIR, LANES), i32),
            vmem((8, NPAIR), i32),
            vmem((8, NPAIR), f32),
            vmem((1, n_alpha), i32),
            vmem((1, n_beta), i32),
            smem((1, n_alpha), i32),
            smem((1, n_beta), i32),
            smem((NBLK, NBLK), i32),
            vmem((SIDE, SIDE, SIDE, n_aux, WIDE), bf16),
            vmem((SIDE, 2, SIDE, SIDE, 8, LANES), bf16),
            vmem((n_alpha * 8, LANES), f32),
            vmem((n_alpha, n_beta), bf16),
            vmem((8 * n_alpha, NPAIR), bf16),
            vmem((chips * n_aux, WIDE), bf16),
            vmem((WIDE, chips * n_aux), bf16),
            vmem((chips * n_aux, 4 * n_alpha), bf16),
            vmem((TALL, 4 * n_alpha), f32),
            vmem((8, n_alpha), f32),
            vmem((8, n_alpha), f32),
            dma((n_aux,)),
            dma((11,)),
            dma((3, 3, SIDE - 1)),
            dma((3, 3, SIDE - 1)),
            dma((3, SIDE - 1)),
            dma((3, SIDE - 1)),
            dma,
            dma,
            dma,
            dma,
        ],
        compiler_params=pltpu.CompilerParams(
            collective_id=0, has_side_effects=True, vmem_limit_bytes=63 << 20
        ),
        name="sigma",
    )(
        vector, integrals.transpose(1, 0, 2).reshape(tall, n_bas), orbitals,
        alpha_addr.T, alpha_sign.T, beta_addr.T, beta_sign.T,
        seg_alpha.reshape(1, -1), seg_beta.reshape(1, -1), allowed,
    )


def solution(mesh):
    rows = P(("grp", "blk"), None)
    placed = (rows, P(("grp", "blk"), None, None)) + (P(),) * 8
    return jax.shard_map(on_device, mesh=mesh, in_specs=placed, out_specs=rows, check_vma=False)
```

```python
import jax
import jax.numpy as jnp
from jax import lax
from jax.experimental import pallas as pl
from jax.experimental.pallas import tpu as pltpu
from jax.sharding import PartitionSpec as P

MESH = pl.DeviceIdType.MESH
SIDE = 4
LANES = 128
NORB = 26
ROWS = 32
NPAIR = NORB * NORB
WIDE = 768
TALL = 680
PART = 256
ORDERS = ((2, 1, 0), (0, 2, 1), (1, 0, 2))
NBLK = 10
CHUNK = 512


def kernel(
    vec_hbm, int_hbm, orb_hbm, aaddr_hbm, asign_hbm, baddr_hbm, bsign_hbm, sega_hbm, segb_hbm, allow_hbm,
    out_ref,
    vec_v, ibuf, orb_v, orb32, orep, wtab, araw, sraw, atab, stab, btab, bsgn, baddr_v, bsign_v,
    sega_v, segb_v, sega_s, segb_s, allow_s,
    fbuf, vbuf, vf32, mbuf, ptt, fmat, fmat_t, tmat, pmat, sig_out, sig_in,
    isem, lsem, f_send, f_recv, v_send, v_recv, s_send, s_recv, c_send, c_recv,
):
    grp = lax.axis_index("grp")
    blk = lax.axis_index("blk")
    core = lax.rem(grp, 2)
    here = (lax.div(grp, 2), lax.div(blk, SIDE), lax.rem(blk, SIDE))
    x, y, z = here
    position = grp * (SIDE * SIDE) + blk
    n_aux = fbuf.shape[3]
    n_alpha = aaddr_hbm.shape[1]
    tall = int_hbm.shape[0]

    def device_at(axis, step):
        spot = list(here)
        spot[axis] = lax.rem(spot[axis] + step, SIDE)
        return (spot[0] * 2 + core, spot[1] * SIDE + spot[2])

    sibling = (x * 2 + (1 - core), blk)

    local = [
        (orb_hbm, orb_v),
        (vec_hbm, vec_v),
        (segb_hbm, segb_v),
        (sega_hbm, sega_s),
        (allow_hbm, allow_s),
        (sega_hbm, sega_v),
        (segb_hbm, segb_s),
        (baddr_hbm.at[:, pl.ds(pl.multiple_of(x * LANES, LANES), LANES)], btab),
        (bsign_hbm.at[:, pl.ds(pl.multiple_of(x * LANES, LANES), LANES)], bsgn),
        (aaddr_hbm, araw),
        (asign_hbm, sraw),
    ]
    local = [pltpu.make_async_copy(src, dst, lsem.at[i]) for i, (src, dst) in enumerate(local)]
    chunks = [(at, min(CHUNK, tall - at)) for at in range(0, tall, CHUNK)]
    slabs = [
        pltpu.make_async_copy(int_hbm.at[pl.ds(at, size), :], ibuf.at[pl.ds(at, size), :], isem.at[i])
        for i, (at, size) in enumerate(chunks)
    ]
    for copy in local[:5]:
        copy.start()
    for copy in slabs:
        copy.start()
    for copy in local[5:]:
        copy.start()

    barrier = pltpu.get_barrier_semaphore()
    for axis in range(3):
        for step in range(1, SIDE):
            pl.semaphore_signal(barrier, inc=1, device_id=device_at(axis, step), device_id_type=MESH)
    pl.semaphore_signal(barrier, inc=1, device_id=sibling, device_id_type=MESH)

    local[0].wait()
    orb32[...] = jnp.zeros_like(orb32)
    orb32[0:NORB, :] = orb_v[...]
    lane = lax.broadcasted_iota(jnp.int32, (1, WIDE), 1)
    first = jnp.zeros((1, WIDE), jnp.int32)
    for i in range(1, NORB + 1):
        first = first + jnp.where(lane >= i * NORB, 1, 0)
    second = lane - NORB * first
    row = lax.broadcasted_iota(jnp.int32, (ROWS, WIDE), 0)
    spread = jnp.where(row == second, 1.0, 0.0).astype(jnp.bfloat16)
    repeat = jnp.where(
        lax.broadcasted_iota(jnp.int32, (ROWS, n_aux * ROWS), 0)
        == lax.rem(lax.broadcasted_iota(jnp.int32, (ROWS, n_aux * ROWS), 1), ROWS),
        1.0, 0.0,
    ).astype(jnp.bfloat16)
    orep[...] = lax.dot_general(
        orb32[...], repeat, (((0,), (0,)), ((), ())), preferred_element_type=jnp.float32
    )
    same = lax.broadcasted_iota(jnp.int32, (n_aux, n_aux * ROWS), 0) == lax.div(
        lax.broadcasted_iota(jnp.int32, (n_aux, n_aux * ROWS), 1), ROWS
    )

    @pl.loop(0, tall // (n_aux * 20))
    def _(i):
        rows = [jnp.where(same, orep[pl.ds(i * 20 + k, 1), :], 0.0) for k in range(20)]
        at = pl.multiple_of(i * (n_aux * 20), n_aux * 20)
        wtab[pl.ds(at, n_aux * 20), :] = jnp.concatenate(rows, axis=0).astype(jnp.bfloat16)

    for copy in local[1:5]:
        copy.wait()
    seg_here = sega_s[0, position]
    row_mask = jnp.zeros(segb_v.shape, jnp.float32)
    for block in range(NBLK):
        row_mask = jnp.where(segb_v[...] == block, allow_s[seg_here, block].astype(jnp.float32), row_mask)
    masked = vec_v[...].astype(jnp.float32) * row_mask
    pieces = [masked[:, i * LANES : (i + 1) * LANES] for i in range(4)] + [jnp.zeros((4, LANES), jnp.float32)]
    vbuf[x, core, y, z] = jnp.concatenate(pieces, axis=0).astype(jnp.bfloat16)

    def v_copy(stage, step):
        place = (
            vbuf.at[x, core, y, z],
            vbuf.at[x, core, y],
            vbuf.at[x, core],
        )[stage]
        return pltpu.make_async_remote_copy(
            src_ref=place, dst_ref=place,
            send_sem=v_send.at[stage, step - 1], recv_sem=v_recv.at[stage, step - 1],
            device_id=device_at(2 - stage, step), device_id_type=MESH,
        )

    def f_copy(part, stage, step):
        order = ORDERS[part]
        index = tuple(slice(None) if axis in order[:stage] else here[axis] for axis in range(3))
        place = fbuf.at[index + (slice(None), pl.ds(part * PART, PART))]
        return pltpu.make_async_remote_copy(
            src_ref=place, dst_ref=place,
            send_sem=f_send.at[part, stage, step - 1], recv_sem=f_recv.at[part, stage, step - 1],
            device_id=device_at(order[stage], step), device_id_type=MESH,
        )

    v_twin = pltpu.make_async_remote_copy(
        src_ref=vbuf.at[:, core], dst_ref=vbuf.at[:, core], send_sem=c_send, recv_sem=c_recv,
        device_id=sibling, device_id_type=MESH,
    )

    def v_start(stage):
        for step in range(1, SIDE):
            v_copy(stage, step).start()

    def v_wait(stage):
        for step in range(1, SIDE):
            v_copy(stage, step).wait_recv()

    def f_start(stage):
        for part in range(3):
            for step in range(1, SIDE):
                f_copy(part, stage, step).start()

    pl.semaphore_wait(barrier, 10)
    v_start(0)

    total = jnp.zeros((ROWS, n_aux * ROWS), jnp.float32)
    for copy, (at, size) in zip(slabs, chunks):
        copy.wait()
        half = lax.dot_general(
            orb32[...], ibuf[at : at + size, :], (((1,), (1,)), ((), ())), preferred_element_type=jnp.float32
        ).astype(jnp.bfloat16)
        total = total + jnp.dot(half, wtab[at : at + size, :], preferred_element_type=jnp.float32)
    whole = lax.dot_general(
        total.astype(jnp.bfloat16), spread, (((0,), (0,)), ((), ())), preferred_element_type=jnp.float32
    )
    whole = jnp.where((row == first)[None], whole.reshape(n_aux, ROWS, WIDE), 0.0)
    fbuf[x, y, z] = jnp.sum(whole, axis=1).astype(jnp.bfloat16)
    f_start(0)

    v_wait(0)
    v_start(1)

    def f_pass(stage):
        for part in range(3):
            for step in range(1, SIDE):
                f_copy(part, stage, step).wait_recv()
            if stage < 2:
                for step in range(1, SIDE):
                    f_copy(part, stage + 1, step).start()

    f_pass(0)
    v_wait(1)
    v_start(2)
    f_pass(1)
    v_wait(2)
    v_twin.start()

    local[9].wait()
    local[10].wait()
    atab[TALL - 8 : TALL, :] = jnp.zeros((8, n_alpha), jnp.int32)
    stab[TALL - 8 : TALL, :] = jnp.zeros((8, n_alpha), jnp.float32)
    atab[0:NPAIR, :] = araw[...]
    stab[0:NPAIR, :] = sraw[...].astype(jnp.float32)

    local[7].wait()
    local[8].wait()
    string = lax.broadcasted_iota(jnp.int32, (8, LANES), 0)
    twin = jnp.where(string < 4, 1 - core, core)
    wanted = twin * (4 * SIDE * SIDE) + blk * 4 + lax.rem(string, 4)
    pick = jnp.where(lax.broadcasted_iota(jnp.int32, (8, LANES), 1) == wanted, 1.0, 0.0).astype(jnp.bfloat16)

    def picked(table):
        return lax.dot_general(
            pick, table.astype(jnp.float32).astype(jnp.bfloat16),
            (((1,), (1,)), ((), ())), preferred_element_type=jnp.float32,
        )

    addr = btab[...]
    high = lax.shift_right_logical(addr, 8)
    baddr_v[...] = (picked(addr - high * 256) + 256.0 * picked(high)).astype(jnp.int32)
    bsign_v[...] = picked(bsgn[...])
    v_twin.wait_recv()
    vf32[...] = vbuf[...].astype(jnp.float32).reshape(n_alpha * 8, LANES)
    for i in range(4):
        mbuf[:, i * LANES : (i + 1) * LANES] = vf32[pl.ds(i, n_alpha, stride=8), :].astype(jnp.bfloat16)

    n_beta = mbuf.shape[1]

    @pl.loop(0, 8, unroll=2)
    def _(i):
        addr = baddr_v[pl.ds(i, 1), :]
        sign = bsign_v[pl.ds(i, 1), :]
        beta = lax.broadcasted_iota(jnp.int32, (n_beta, NPAIR), 0)
        table = jnp.where(beta == addr, sign, 0.0).astype(jnp.bfloat16)
        ptt[pl.ds(pl.multiple_of(i * n_alpha, n_alpha), n_alpha), :] = jnp.dot(
            mbuf[...], table, preferred_element_type=jnp.float32
        ).astype(jnp.bfloat16)

    f_pass(2)
    count = fmat.shape[0]
    fmat[...] = fbuf[...].astype(jnp.float32).reshape(count, WIDE).astype(jnp.bfloat16)
    fmat_t[...] = fmat[...].T

    def half_sigma(half):
        rows = 4 * n_alpha
        tmat[...] = lax.dot_general(
            fmat[:, 0:NPAIR], ptt[half * rows : (half + 1) * rows, :],
            (((1,), (1,)), ((), ())), preferred_element_type=jnp.float32,
        ).astype(jnp.bfloat16)
        pmat[...] = jnp.dot(fmat_t[0:TALL, :], tmat[...], preferred_element_type=jnp.float32)

        def add_rows(i, totals):
            at = pl.ds(pl.multiple_of(i * 8, 8), 8)
            index = atab[at, :]
            sign = stab[at, :]
            return tuple(
                total + sign * jnp.take_along_axis(
                    pmat[at, b * n_alpha : (b + 1) * n_alpha], index, axis=1, mode="promise_in_bounds"
                )
                for b, total in enumerate(totals)
            )

        totals = lax.fori_loop(0, TALL // 8, add_rows, (jnp.zeros((8, n_alpha), jnp.float32),) * 4, unroll=True)
        return jnp.concatenate([jnp.sum(total, axis=0, keepdims=True) for total in totals], axis=0)

    sig_out[0:4, :] = half_sigma(0)
    s_copy = pltpu.make_async_remote_copy(
        src_ref=sig_out, dst_ref=sig_in, send_sem=s_send, recv_sem=s_recv,
        device_id=sibling, device_id_type=MESH,
    )
    s_copy.start()
    mine = half_sigma(1)
    local[5].wait()
    local[6].wait()
    column = []
    for b in range(4):
        seg = segb_s[0, position * 4 + b]
        mask = jnp.zeros((1, n_alpha), jnp.float32)
        for block in range(NBLK):
            mask = jnp.where(sega_v[...] == block, allow_s[block, seg].astype(jnp.float32), mask)
        column.append(mask)
    s_copy.wait_recv()
    out_ref[...] = (mine + sig_in[0:4, :]) * jnp.concatenate(column, axis=0)

    for stage in range(3):
        for step in range(1, SIDE):
            v_copy(stage, step).wait_send()
            for part in range(3):
                f_copy(part, stage, step).wait_send()
    v_twin.wait_send()
    s_copy.wait_send()


def on_device(
    vector, integrals, orbitals, alpha_addr, alpha_sign, beta_addr, beta_sign, seg_alpha, seg_beta, allowed
):
    n_aux, n_bas, _ = integrals.shape
    n_alpha = alpha_addr.shape[0]
    tall = n_aux * n_bas
    n_beta = beta_addr.shape[0]
    bf16, f32, i32 = jnp.bfloat16, jnp.float32, jnp.int32
    vmem, smem, dma = pltpu.VMEM, pltpu.SMEM, pltpu.SemaphoreType.DMA
    chips = SIDE**3
    return pl.pallas_call(
        kernel,
        out_shape=jax.ShapeDtypeStruct((n_beta // (2 * chips), n_alpha), f32),
        in_specs=[pl.BlockSpec(memory_space=pltpu.HBM)] * 10,
        out_specs=pl.BlockSpec(memory_space=pltpu.VMEM),
        scratch_shapes=[
            vmem((1, n_beta), bf16),
            vmem((tall, n_bas), bf16),
            vmem((NORB, n_bas), bf16),
            vmem((ROWS, n_bas), bf16),
            vmem((n_bas, n_aux * ROWS), f32),
            vmem((tall, n_aux * ROWS), bf16),
            vmem((NPAIR, n_alpha), i32),
            vmem((NPAIR, n_alpha), i32),
            vmem((TALL, n_alpha), i32),
            vmem((TALL, n_alpha), f32),
            vmem((NPAIR, LANES), i32),
            vmem((NPAIR, LANES), i32),
            vmem((8, NPAIR), i32),
            vmem((8, NPAIR), f32),
            vmem((1, n_alpha), i32),
            vmem((1, n_beta), i32),
            smem((1, n_alpha), i32),
            smem((1, n_beta), i32),
            smem((NBLK, NBLK), i32),
            vmem((SIDE, SIDE, SIDE, n_aux, WIDE), bf16),
            vmem((SIDE, 2, SIDE, SIDE, 8, LANES), bf16),
            vmem((n_alpha * 8, LANES), f32),
            vmem((n_alpha, n_beta), bf16),
            vmem((8 * n_alpha, NPAIR), bf16),
            vmem((chips * n_aux, WIDE), bf16),
            vmem((WIDE, chips * n_aux), bf16),
            vmem((chips * n_aux, 4 * n_alpha), bf16),
            vmem((TALL, 4 * n_alpha), f32),
            vmem((8, n_alpha), f32),
            vmem((8, n_alpha), f32),
            dma((n_aux,)),
            dma((11,)),
            dma((3, 3, SIDE - 1)),
            dma((3, 3, SIDE - 1)),
            dma((3, SIDE - 1)),
            dma((3, SIDE - 1)),
            dma,
            dma,
            dma,
            dma,
        ],
        compiler_params=pltpu.CompilerParams(
            collective_id=0, has_side_effects=True, vmem_limit_bytes=63 << 20
        ),
        name="sigma",
    )(
        vector, integrals.transpose(1, 0, 2).reshape(tall, n_bas), orbitals,
        alpha_addr.T, alpha_sign.T, beta_addr.T, beta_sign.T,
        seg_alpha.reshape(1, -1), seg_beta.reshape(1, -1), allowed,
    )


def solution(mesh):
    rows = P(("grp", "blk"), None)
    placed = (rows, P(("grp", "blk"), None, None)) + (P(),) * 8
    return jax.shard_map(on_device, mesh=mesh, in_specs=placed, out_specs=rows, check_vma=False)
```

```python
import jax
import jax.numpy as jnp
from jax import lax
from jax.experimental import pallas as pl
from jax.experimental.pallas import tpu as pltpu
from jax.sharding import PartitionSpec as P

MESH = pl.DeviceIdType.MESH
SIDE = 4
LANES = 128
NORB = 26
ROWS = 32
NPAIR = NORB * NORB
WIDE = 768
TALL = 680
PART = 256
NBLK = 10
HALF = 256
STEPS = sorted(
    [(a, b, c) for a in range(SIDE) for b in range(SIDE) for c in range(SIDE)
     if (a, b, c) != (0, 0, 0) and 0 in (a, b, c)],
    key=lambda step: -sum(min(k, SIDE - k) for k in step),
)
PLANES = ((1, 2, 0), (2, 0, 1), (0, 1, 2))
CHUNK = 512


def kernel(
    vec_hbm, int_hbm, orb_hbm, aaddr_hbm, asign_hbm, baddr_hbm, bsign_hbm, sega_hbm, segb_hbm, allow_hbm,
    out_ref,
    vec_v, ibuf, orb_v, orb32, orep, wtab, araw, sraw, atab, stab, btab, bsgn, baddr_v, bsign_v,
    sega_v, segb_v, segb_s, allow_s, allow_v, allow_b, mask,
    fbuf, vbuf, vf32, mbuf, chosen, ptt, fmat, tmat, pmat, sig_out, sig_in,
    isem, lsem, f_send, f_recv, v_send, v_recv, s_send, s_recv, c_send, c_recv,
):
    grp = lax.axis_index("grp")
    blk = lax.axis_index("blk")
    core = lax.rem(grp, 2)
    here = (lax.div(grp, 2), lax.div(blk, SIDE), lax.rem(blk, SIDE))
    x, y, z = here
    position = grp * (SIDE * SIDE) + blk
    n_aux = fbuf.shape[3]
    n_alpha = aaddr_hbm.shape[1]
    tall = int_hbm.shape[0]

    def device_at(step):
        spot = [lax.rem(at + k, SIDE) for at, k in zip(here, step)]
        return (spot[0] * 2 + core, spot[1] * SIDE + spot[2])

    sibling = (x * 2 + (1 - core), blk)

    local = [
        (orb_hbm, orb_v),
        (vec_hbm, vec_v),
        (segb_hbm, segb_v),
        (sega_hbm, sega_v),
        (allow_hbm, allow_s),
        (allow_hbm, allow_v),
        (segb_hbm, segb_s),
        (baddr_hbm.at[:, pl.ds(pl.multiple_of(x * LANES, LANES), LANES)], btab),
        (bsign_hbm.at[:, pl.ds(pl.multiple_of(x * LANES, LANES), LANES)], bsgn),
        (aaddr_hbm, araw),
        (asign_hbm, sraw),
    ]
    local = [pltpu.make_async_copy(src, dst, lsem.at[i]) for i, (src, dst) in enumerate(local)]
    chunks = [(at, min(CHUNK, tall - at)) for at in range(0, tall, CHUNK)]
    slabs = [
        pltpu.make_async_copy(int_hbm.at[pl.ds(at, size), :], ibuf.at[pl.ds(at, size), :], isem.at[i])
        for i, (at, size) in enumerate(chunks)
    ]
    local[0].start()
    for copy in slabs:
        copy.start()
    local[1].start()

    barrier = pltpu.get_barrier_semaphore()
    for step in STEPS:
        pl.semaphore_signal(barrier, inc=1, device_id=device_at(step), device_id_type=MESH)
    pl.semaphore_signal(barrier, inc=1, device_id=sibling, device_id_type=MESH)

    local[0].wait()
    orb32[...] = jnp.zeros_like(orb32)
    orb32[0:NORB, :] = orb_v[...]
    lane = lax.broadcasted_iota(jnp.int32, (1, WIDE), 1)
    first = jnp.zeros((1, WIDE), jnp.int32)
    for i in range(1, NORB + 1):
        first = first + jnp.where(lane >= i * NORB, 1, 0)
    second = lane - NORB * first
    row = lax.broadcasted_iota(jnp.int32, (ROWS, WIDE), 0)
    spread = jnp.where(row == second, 1.0, 0.0).astype(jnp.bfloat16)
    repeat = jnp.where(
        lax.broadcasted_iota(jnp.int32, (ROWS, n_aux * ROWS), 0)
        == lax.rem(lax.broadcasted_iota(jnp.int32, (ROWS, n_aux * ROWS), 1), ROWS),
        1.0, 0.0,
    ).astype(jnp.bfloat16)
    orep[...] = lax.dot_general(
        orb32[...], repeat, (((0,), (0,)), ((), ())), preferred_element_type=jnp.float32
    )
    same = lax.broadcasted_iota(jnp.int32, (n_aux, n_aux * ROWS), 0) == lax.div(
        lax.broadcasted_iota(jnp.int32, (n_aux, n_aux * ROWS), 1), ROWS
    )

    @pl.loop(0, tall // (n_aux * 20))
    def _(i):
        rows = [jnp.where(same, orep[pl.ds(i * 20 + k, 1), :], 0.0) for k in range(20)]
        at = pl.multiple_of(i * (n_aux * 20), n_aux * 20)
        wtab[pl.ds(at, n_aux * 20), :] = jnp.concatenate(rows, axis=0).astype(jnp.bfloat16)

    def remote(place, send, recv, target):
        return pltpu.make_async_remote_copy(
            src_ref=place, dst_ref=place, send_sem=send, recv_sem=recv, device_id=target, device_id_type=MESH
        )

    v_copies = [
        remote(vbuf.at[x, core, y, z], v_send.at[n], v_recv.at[n], device_at(step))
        for n, step in enumerate(STEPS) if step[0] == 0
    ]
    v_later = [
        remote(vbuf.at[x, core], v_send.at[len(STEPS) + k], v_recv.at[len(STEPS) + k], device_at((k, 0, 0)))
        for k in (2, 1, 3)
    ]
    v_twin = remote(vbuf.at[:, core], c_send, c_recv, sibling)
    f_copies, later = [[], [], []], [[], [], []]
    for part, (_, _, across) in enumerate(PLANES):
        lanes = pl.ds(part * PART, PART)
        for step in STEPS:
            if step[across] == 0:
                n = len(f_copies[part])
                f_copies[part].append(
                    remote(
                        fbuf.at[x, y, z, :, lanes], f_send.at[part, n], f_recv.at[part, n], device_at(step)
                    )
                )
        plane = tuple(here[axis] if axis == across else slice(None) for axis in range(3))
        for n, k in enumerate((2, 1, 3)):
            step = tuple(k if axis == across else 0 for axis in range(3))
            later[part].append(
                remote(
                    fbuf.at[plane + (slice(None), lanes)], f_send.at[part, 15 + n], f_recv.at[part, 15 + n],
                    device_at(step),
                )
            )
    total = jnp.zeros((ROWS, n_aux * ROWS), jnp.float32)
    for n, (at, size) in enumerate(chunks):
        if n % 4 == 0:
            for copy in slabs[n : n + 4]:
                copy.wait()
        half = lax.dot_general(
            orb32[...], ibuf[at : at + size, :], (((1,), (1,)), ((), ())), preferred_element_type=jnp.float32
        ).astype(jnp.bfloat16)
        total = total + jnp.dot(half, wtab[at : at + size, :], preferred_element_type=jnp.float32)
    local[1].wait()
    row_f = vec_v[...].astype(jnp.float32)
    pieces = [row_f[:, i * LANES : (i + 1) * LANES] for i in range(4)]
    vbuf[x, core, y, z] = jnp.concatenate(pieces, axis=0).astype(jnp.bfloat16)

    pl.semaphore_wait(barrier, len(STEPS) + 1)
    for copy in v_copies:
        copy.start()
    whole = lax.dot_general(
        total.astype(jnp.bfloat16), spread, (((0,), (0,)), ((), ())), preferred_element_type=jnp.float32
    )
    whole = jnp.where((row == first)[None], whole.reshape(n_aux, ROWS, WIDE), 0.0)
    fbuf[x, y, z] = jnp.sum(whole, axis=1).astype(jnp.bfloat16)


    for together in zip(*f_copies):
        for copy in together:
            copy.start()

    for copy in local[2:]:
        copy.start()

    for copy in local[2:7]:
        copy.wait()
    n_beta = mask.shape[1]
    allow_b[...] = jnp.zeros_like(allow_b)
    allow_b[0:NBLK, 0:NBLK] = allow_v[...].astype(jnp.float32)
    block_a = lax.broadcasted_iota(jnp.int32, (ROWS, n_alpha), 0) == sega_v[...]
    block_b = lax.broadcasted_iota(jnp.int32, (ROWS, n_beta), 0) == segb_v[...]
    by_block = jnp.dot(
        allow_b[...].astype(jnp.bfloat16), jnp.where(block_b, 1.0, 0.0).astype(jnp.bfloat16),
        preferred_element_type=jnp.float32,
    ).astype(jnp.bfloat16)
    mask[...] = lax.dot_general(
        jnp.where(block_a, 1.0, 0.0).astype(jnp.bfloat16), by_block,
        (((0,), (0,)), ((), ())), preferred_element_type=jnp.float32,
    )

    local[9].wait()
    local[10].wait()
    atab[TALL - 8 : TALL, :] = jnp.zeros((8, n_alpha), jnp.int32)
    stab[TALL - 8 : TALL, :] = jnp.zeros((8, n_alpha), jnp.float32)
    atab[0:NPAIR, :] = araw[...]
    stab[0:NPAIR, :] = sraw[...].astype(jnp.float32)

    local[7].wait()
    local[8].wait()
    string = lax.broadcasted_iota(jnp.int32, (8, LANES), 0)
    twin = jnp.where(string < 4, 1 - core, core)
    wanted = twin * (4 * SIDE * SIDE) + blk * 4 + lax.rem(string, 4)
    pick = jnp.where(lax.broadcasted_iota(jnp.int32, (8, LANES), 1) == wanted, 1.0, 0.0).astype(jnp.bfloat16)

    def picked(table):
        return lax.dot_general(
            pick, table.astype(jnp.float32).astype(jnp.bfloat16),
            (((1,), (1,)), ((), ())), preferred_element_type=jnp.float32,
        )

    addr = btab[...]
    high = lax.shift_right_logical(addr, 8)
    baddr_v[...] = (picked(addr - high * 256) + 256.0 * picked(high)).astype(jnp.int32)
    bsign_v[...] = picked(bsgn[...])

    @pl.loop(0, 8)
    def _(i):
        addr = lax.rem(baddr_v[pl.ds(i, 1), :], HALF)
        place = lax.broadcasted_iota(jnp.int32, (HALF, NPAIR), 0)
        chosen[i] = jnp.where(place == addr, bsign_v[pl.ds(i, 1), :], 0.0).astype(jnp.bfloat16)
    for copy in v_copies:
        copy.wait_recv()
    for copy in v_later:
        copy.start()
    for part in range(3):
        for copy in f_copies[part]:
            copy.wait_recv()
        for copy in later[part]:
            copy.start()

    for copy in v_later:
        copy.wait_recv()
    v_twin.start()
    v_twin.wait_recv()
    vf32[:, 0:4, :] = vbuf[...].astype(jnp.float32).reshape(n_alpha, 4, LANES)
    for i in range(4):
        lanes = slice(i * LANES, (i + 1) * LANES)
        at, to = (i // 2) * n_alpha, (i % 2) * LANES
        mbuf[at : at + n_alpha, to : to + LANES] = (vf32[:, i, :] * mask[:, lanes]).astype(jnp.bfloat16)
    for i in range(8):
        both = jnp.dot(mbuf[...], chosen[i], preferred_element_type=jnp.float32)
        ptt[i * n_alpha : (i + 1) * n_alpha, :] = jnp.where(
            baddr_v[i : i + 1, :] >= HALF, both[n_alpha:, :], both[:n_alpha, :]
        ).astype(jnp.bfloat16)

    for part in range(3):
        for copy in later[part]:
            copy.wait_recv()
    count = fmat.shape[0]
    fmat[...] = fbuf[...].astype(jnp.float32).reshape(count, WIDE).astype(jnp.bfloat16)
    tmat[...] = lax.dot_general(
        fmat[:, 0:NPAIR], ptt[...], (((1,), (1,)), ((), ())), preferred_element_type=jnp.float32
    ).astype(jnp.bfloat16)

    rows = 4 * n_alpha
    for half in range(2):
        pmat[half] = lax.dot_general(
            fmat[...], tmat[:, half * rows : (half + 1) * rows],
            (((0,), (0,)), ((), ())), preferred_element_type=jnp.float32,
        )

    def half_sigma(half):
        def add_rows(i, totals):
            at = pl.ds(pl.multiple_of(i * 8, 8), 8)
            index = atab[at, :]
            sign = stab[at, :]
            return tuple(
                total + sign * jnp.take_along_axis(
                    pmat[half, at, b * n_alpha : (b + 1) * n_alpha], index, axis=1, mode="promise_in_bounds"
                )
                for b, total in enumerate(totals)
            )

        totals = lax.fori_loop(0, TALL // 8, add_rows, (jnp.zeros((8, n_alpha), jnp.float32),) * 4, unroll=True)
        return jnp.concatenate([jnp.sum(total, axis=0, keepdims=True) for total in totals], axis=0)

    sig_out[0:4, :] = half_sigma(0)
    s_copy = pltpu.make_async_remote_copy(
        src_ref=sig_out, dst_ref=sig_in, send_sem=s_send, recv_sem=s_recv, device_id=sibling, device_id_type=MESH
    )
    s_copy.start()
    mine = half_sigma(1)
    column = []
    for b in range(4):
        seg = segb_s[0, position * 4 + b]
        kept = jnp.zeros((1, n_alpha), jnp.float32)
        for block in range(NBLK):
            kept = jnp.where(sega_v[...] == block, allow_s[block, seg].astype(jnp.float32), kept)
        column.append(kept)
    s_copy.wait_recv()
    out_ref[...] = (mine + sig_in[0:4, :]) * jnp.concatenate(column, axis=0)

    for copy in v_copies + v_later:
        copy.wait_send()
    for part in range(3):
        for copy in f_copies[part] + later[part]:
            copy.wait_send()
    v_twin.wait_send()
    s_copy.wait_send()


def on_device(
    vector, integrals, orbitals, alpha_addr, alpha_sign, beta_addr, beta_sign, seg_alpha, seg_beta, allowed
):
    n_aux, n_bas, _ = integrals.shape
    n_alpha = alpha_addr.shape[0]
    tall = n_aux * n_bas
    n_beta = beta_addr.shape[0]
    bf16, f32, i32 = jnp.bfloat16, jnp.float32, jnp.int32
    vmem, smem, dma = pltpu.VMEM, pltpu.SMEM, pltpu.SemaphoreType.DMA
    chips = SIDE**3
    return pl.pallas_call(
        kernel,
        out_shape=pltpu.VMEM((n_beta // (2 * chips), n_alpha), f32),
        in_specs=[pl.BlockSpec(memory_space=pltpu.HBM)] * 10,
        out_specs=pl.BlockSpec(memory_space=pltpu.VMEM),
        scratch_shapes=[
            vmem((1, n_beta), bf16),
            vmem((tall, n_bas), bf16),
            vmem((NORB, n_bas), bf16),
            vmem((ROWS, n_bas), bf16),
            vmem((n_bas, n_aux * ROWS), f32),
            vmem((tall, n_aux * ROWS), bf16),
            vmem((NPAIR, n_alpha), i32),
            vmem((NPAIR, n_alpha), i32),
            vmem((TALL, n_alpha), i32),
            vmem((TALL, n_alpha), f32),
            vmem((NPAIR, LANES), i32),
            vmem((NPAIR, LANES), i32),
            vmem((8, NPAIR), i32),
            vmem((8, NPAIR), f32),
            vmem((1, n_alpha), i32),
            vmem((1, n_beta), i32),
            smem((1, n_beta), i32),
            smem((NBLK, NBLK), i32),
            vmem((NBLK, NBLK), i32),
            vmem((ROWS, ROWS), f32),
            vmem((n_alpha, n_beta), f32),
            vmem((SIDE, SIDE, SIDE, n_aux, WIDE), bf16),
            vmem((SIDE, 2, SIDE, SIDE, 4, LANES), bf16),
            vmem((n_alpha, 8, LANES), f32),
            vmem((2 * n_alpha, HALF), bf16),
            vmem((8, HALF, NPAIR), bf16),
            vmem((8 * n_alpha, NPAIR), bf16),
            vmem((chips * n_aux, WIDE), bf16),
            vmem((chips * n_aux, 8 * n_alpha), bf16),
            vmem((2, WIDE, 4 * n_alpha), f32),
            vmem((8, n_alpha), f32),
            vmem((8, n_alpha), f32),
            dma((n_aux,)),
            dma((11,)),
            dma((3, 18)),
            dma((3, 18)),
            dma((len(STEPS) + SIDE,)),
            dma((len(STEPS) + SIDE,)),
            dma,
            dma,
            dma,
            dma,
        ],
        compiler_params=pltpu.CompilerParams(
            collective_id=0, has_side_effects=True, vmem_limit_bytes=63 << 20
        ),
        name="sigma",
    )(
        vector, integrals.transpose(1, 0, 2).reshape(tall, n_bas), orbitals,
        alpha_addr.T, alpha_sign.T, beta_addr.T, beta_sign.T,
        seg_alpha.reshape(1, -1), seg_beta.reshape(1, -1), allowed,
    )


def solution(mesh):
    rows = P(("grp", "blk"), None)
    placed = (rows, P(("grp", "blk"), None, None)) + (P(),) * 8
    return jax.shard_map(on_device, mesh=mesh, in_specs=placed, out_specs=rows, check_vma=False)
```

```python
import jax
import jax.numpy as jnp
from jax import lax
from jax.experimental import pallas as pl
from jax.experimental.pallas import tpu as pltpu
from jax.sharding import PartitionSpec as P

MESH = pl.DeviceIdType.MESH
SIDE = 4
LANES = 128
NORB = 26
ROWS = 32
NPAIR = NORB * NORB
WIDE = 768
TALL = 680
PART = 256
NBLK = 10
HALF = 256
STEPS = sorted(
    [(a, b, c) for a in range(SIDE) for b in range(SIDE) for c in range(SIDE)
     if (a, b, c) != (0, 0, 0) and 0 in (a, b, c)],
    key=lambda step: -sum(min(k, SIDE - k) for k in step),
)
PLANES = ((1, 2, 0), (2, 0, 1), (0, 1, 2))
CHUNK = 512


def kernel(
    vec_hbm, int_hbm, orb_hbm, aaddr_hbm, asign_hbm, baddr_hbm, bsign_hbm, sega_hbm, segb_hbm, allow_hbm,
    out_ref,
    vec_v, ibuf, orb_v, orb32, orep, wtab, halves, araw, sraw, atab, stab, btab, bsgn, baddr_v, bsign_v,
    sega_v, segb_v, segb_s, allow_s, allow_v, allow_b, mask,
    fbuf, vbuf, vf32, mbuf, chosen, ptt, fmat, tmat, pmat, sig_out, sig_in,
    isem, lsem, f_send, f_recv, v_send, v_recv, s_send, s_recv,
):
    grp = lax.axis_index("grp")
    blk = lax.axis_index("blk")
    core = lax.rem(grp, 2)
    here = (lax.div(grp, 2), lax.div(blk, SIDE), lax.rem(blk, SIDE))
    x, y, z = here
    position = grp * (SIDE * SIDE) + blk
    n_aux = fbuf.shape[3]
    n_alpha = aaddr_hbm.shape[1]
    tall = int_hbm.shape[0]

    def device_at(step, other=False):
        spot = [lax.rem(at + k, SIDE) for at, k in zip(here, step)]
        return (spot[0] * 2 + (1 - core if other else core), spot[1] * SIDE + spot[2])

    sibling = (x * 2 + (1 - core), blk)

    local = [
        (orb_hbm, orb_v),
        (vec_hbm, vec_v),
        (segb_hbm, segb_v),
        (sega_hbm, sega_v),
        (allow_hbm, allow_s),
        (allow_hbm, allow_v),
        (segb_hbm, segb_s),
        (baddr_hbm.at[:, pl.ds(pl.multiple_of(x * LANES, LANES), LANES)], btab),
        (bsign_hbm.at[:, pl.ds(pl.multiple_of(x * LANES, LANES), LANES)], bsgn),
        (aaddr_hbm, araw),
        (asign_hbm, sraw),
    ]
    local = [pltpu.make_async_copy(src, dst, lsem.at[i]) for i, (src, dst) in enumerate(local)]
    chunks = [(at, min(CHUNK, tall - at)) for at in range(0, tall, CHUNK)]
    slabs = [
        pltpu.make_async_copy(int_hbm.at[pl.ds(at, size), :], ibuf.at[pl.ds(at, size), :], isem.at[i])
        for i, (at, size) in enumerate(chunks)
    ]
    local[0].start()
    for copy in slabs:
        copy.start()
    local[1].start()

    barrier = pltpu.get_barrier_semaphore()
    for step in STEPS:
        pl.semaphore_signal(barrier, inc=1, device_id=device_at(step), device_id_type=MESH)
    for k in (2, 1, 3, 0):
        pl.semaphore_signal(barrier, inc=1, device_id=device_at((k, 0, 0), True), device_id_type=MESH)

    local[0].wait()
    orb32[...] = jnp.zeros_like(orb32)
    orb32[0:NORB, :] = orb_v[...]

    def remote(place, send, recv, target):
        return pltpu.make_async_remote_copy(
            src_ref=place, dst_ref=place, send_sem=send, recv_sem=recv, device_id=target, device_id_type=MESH
        )

    v_copies = [
        remote(vbuf.at[x, core, y, z], v_send.at[n], v_recv.at[n], device_at(step))
        for n, step in enumerate(STEPS) if step[0] == 0
    ]
    v_later = [
        remote(
            vbuf.at[x, core], v_send.at[len(STEPS) + n], v_recv.at[len(STEPS) + n], device_at((k, 0, 0), other)
        )
        for n, (k, other) in enumerate(((2, False), (2, True), (1, False), (3, False), (1, True), (3, True), (0, True)))
    ]
    f_copies, later = [[], [], []], [[], [], []]
    for part, (_, _, across) in enumerate(PLANES):
        lanes = pl.ds(part * PART, PART)
        for step in STEPS:
            if step[across] == 0:
                n = len(f_copies[part])
                f_copies[part].append(
                    remote(
                        fbuf.at[x, y, z, :, lanes], f_send.at[part, n], f_recv.at[part, n], device_at(step)
                    )
                )
        plane = tuple(here[axis] if axis == across else slice(None) for axis in range(3))
        for n, k in enumerate((2, 1, 3)):
            step = tuple(k if axis == across else 0 for axis in range(3))
            later[part].append(
                remote(
                    fbuf.at[plane + (slice(None), lanes)], f_send.at[part, 15 + n], f_recv.at[part, 15 + n],
                    device_at(step),
                )
            )
    def first_half(at, size):
        halves[:, at : at + size] = lax.dot_general(
            orb32[...], ibuf[at : at + size, :], (((1,), (1,)), ((), ())), preferred_element_type=jnp.float32
        ).astype(jnp.bfloat16)

    for copy in slabs[:4]:
        copy.wait()
    for at, size in chunks[:4]:
        first_half(at, size)
    lane = lax.broadcasted_iota(jnp.int32, (1, WIDE), 1)
    first = jnp.zeros((1, WIDE), jnp.int32)
    for i in range(1, NORB + 1):
        first = first + jnp.where(lane >= i * NORB, 1, 0)
    second = lane - NORB * first
    row = lax.broadcasted_iota(jnp.int32, (ROWS, WIDE), 0)
    spread = jnp.where(row == second, 1.0, 0.0).astype(jnp.bfloat16)
    repeat = jnp.where(
        lax.broadcasted_iota(jnp.int32, (ROWS, n_aux * ROWS), 0)
        == lax.rem(lax.broadcasted_iota(jnp.int32, (ROWS, n_aux * ROWS), 1), ROWS),
        1.0, 0.0,
    ).astype(jnp.bfloat16)
    orep[...] = lax.dot_general(
        orb32[...], repeat, (((0,), (0,)), ((), ())), preferred_element_type=jnp.float32
    )
    same = lax.broadcasted_iota(jnp.int32, (n_aux, n_aux * ROWS), 0) == lax.div(
        lax.broadcasted_iota(jnp.int32, (n_aux, n_aux * ROWS), 1), ROWS
    )

    @pl.loop(0, tall // (n_aux * 20), unroll=True)
    def _(i):
        rows = [jnp.where(same, orep[pl.ds(i * 20 + k, 1), :], 0.0) for k in range(20)]
        at = pl.multiple_of(i * (n_aux * 20), n_aux * 20)
        wtab[pl.ds(at, n_aux * 20), :] = jnp.concatenate(rows, axis=0).astype(jnp.bfloat16)

    for copy in slabs[4:]:
        copy.wait()
    for at, size in chunks[4:]:
        first_half(at, size)
    total = jnp.dot(halves[...], wtab[...], preferred_element_type=jnp.float32)

    local[1].wait()
    row_f = vec_v[...].astype(jnp.float32)
    pieces = [row_f[:, i * LANES : (i + 1) * LANES] for i in range(4)]
    vbuf[x, core, y, z] = jnp.concatenate(pieces, axis=0).astype(jnp.bfloat16)

    pl.semaphore_wait(barrier, len(STEPS) + SIDE)
    for copy in v_copies:
        copy.start()
    whole = lax.dot_general(
        total.astype(jnp.bfloat16), spread, (((0,), (0,)), ((), ())), preferred_element_type=jnp.float32
    )
    whole = jnp.where((row == first)[None], whole.reshape(n_aux, ROWS, WIDE), 0.0)
    fbuf[x, y, z] = jnp.sum(whole, axis=1).astype(jnp.bfloat16)


    for together in zip(*f_copies):
        for copy in together:
            copy.start()

    for copy in local[2:]:
        copy.start()

    for copy in local[2:7]:
        copy.wait()
    n_beta = mask.shape[1]
    allow_b[...] = jnp.zeros_like(allow_b)
    allow_b[0:NBLK, 0:NBLK] = allow_v[...].astype(jnp.float32)
    block_a = lax.broadcasted_iota(jnp.int32, (ROWS, n_alpha), 0) == sega_v[...]
    block_b = lax.broadcasted_iota(jnp.int32, (ROWS, n_beta), 0) == segb_v[...]
    by_block = jnp.dot(
        allow_b[...].astype(jnp.bfloat16), jnp.where(block_b, 1.0, 0.0).astype(jnp.bfloat16),
        preferred_element_type=jnp.float32,
    ).astype(jnp.bfloat16)
    mask[...] = lax.dot_general(
        jnp.where(block_a, 1.0, 0.0).astype(jnp.bfloat16), by_block,
        (((0,), (0,)), ((), ())), preferred_element_type=jnp.float32,
    )

    local[9].wait()
    local[10].wait()
    atab[TALL - 8 : TALL, :] = jnp.zeros((8, n_alpha), jnp.int32)
    stab[TALL - 8 : TALL, :] = jnp.zeros((8, n_alpha), jnp.float32)
    atab[0:NPAIR, :] = araw[...]
    stab[0:NPAIR, :] = sraw[...].astype(jnp.float32)

    local[7].wait()
    local[8].wait()
    string = lax.broadcasted_iota(jnp.int32, (8, LANES), 0)
    twin = jnp.where(string < 4, 1 - core, core)
    wanted = twin * (4 * SIDE * SIDE) + blk * 4 + lax.rem(string, 4)
    pick = jnp.where(lax.broadcasted_iota(jnp.int32, (8, LANES), 1) == wanted, 1.0, 0.0).astype(jnp.bfloat16)

    def picked(table):
        return lax.dot_general(
            pick, table.astype(jnp.float32).astype(jnp.bfloat16),
            (((1,), (1,)), ((), ())), preferred_element_type=jnp.float32,
        )

    addr = btab[...]
    high = lax.shift_right_logical(addr, 8)
    baddr_v[...] = (picked(addr - high * 256) + 256.0 * picked(high)).astype(jnp.int32)
    bsign_v[...] = picked(bsgn[...])

    @pl.loop(0, 8)
    def _(i):
        addr = lax.rem(baddr_v[pl.ds(i, 1), :], HALF)
        place = lax.broadcasted_iota(jnp.int32, (HALF, NPAIR), 0)
        chosen[i] = jnp.where(place == addr, bsign_v[pl.ds(i, 1), :], 0.0).astype(jnp.bfloat16)
    for copy in v_copies:
        copy.wait_recv()
    for copy in v_later:
        copy.start()
    for part in range(3):
        for copy in f_copies[part]:
            copy.wait_recv()
        for copy in later[part]:
            copy.start()

    for copy in v_later:
        copy.wait_recv()
    vf32[:, 0:4, :] = vbuf[...].astype(jnp.float32).reshape(n_alpha, 4, LANES)
    for i in range(4):
        lanes = slice(i * LANES, (i + 1) * LANES)
        at, to = (i // 2) * n_alpha, (i % 2) * LANES
        mbuf[at : at + n_alpha, to : to + LANES] = (vf32[:, i, :] * mask[:, lanes]).astype(jnp.bfloat16)
    for i in range(8):
        both = jnp.dot(mbuf[...], chosen[i], preferred_element_type=jnp.float32)
        ptt[i * n_alpha : (i + 1) * n_alpha, :] = jnp.where(
            baddr_v[i : i + 1, :] >= HALF, both[n_alpha:, :], both[:n_alpha, :]
        ).astype(jnp.bfloat16)

    for part in range(3):
        for copy in later[part]:
            copy.wait_recv()
    count = fmat.shape[0]
    fmat[...] = fbuf[...].astype(jnp.float32).reshape(count, WIDE).astype(jnp.bfloat16)
    tmat[...] = lax.dot_general(
        fmat[:, 0:NPAIR], ptt[...], (((1,), (1,)), ((), ())), preferred_element_type=jnp.float32
    ).astype(jnp.bfloat16)

    rows = 4 * n_alpha
    for half in range(2):
        pmat[half] = lax.dot_general(
            fmat[...], tmat[:, half * rows : (half + 1) * rows],
            (((0,), (0,)), ((), ())), preferred_element_type=jnp.float32,
        )

    def half_sigma(half):
        def add_rows(i, totals):
            at = pl.ds(pl.multiple_of(i * 8, 8), 8)
            index = atab[at, :]
            sign = stab[at, :]
            return tuple(
                total + sign * jnp.take_along_axis(
                    pmat[half, at, b * n_alpha : (b + 1) * n_alpha], index, axis=1, mode="promise_in_bounds"
                )
                for b, total in enumerate(totals)
            )

        totals = lax.fori_loop(0, TALL // 8, add_rows, (jnp.zeros((8, n_alpha), jnp.float32),) * 4, unroll=True)
        return jnp.concatenate([jnp.sum(total, axis=0, keepdims=True) for total in totals], axis=0)

    sig_out[0:4, :] = half_sigma(0)
    s_copy = pltpu.make_async_remote_copy(
        src_ref=sig_out, dst_ref=sig_in, send_sem=s_send, recv_sem=s_recv, device_id=sibling, device_id_type=MESH
    )
    s_copy.start()
    mine = half_sigma(1)
    column = []
    for b in range(4):
        seg = segb_s[0, position * 4 + b]
        kept = jnp.zeros((1, n_alpha), jnp.float32)
        for block in range(NBLK):
            kept = jnp.where(sega_v[...] == block, allow_s[block, seg].astype(jnp.float32), kept)
        column.append(kept)
    s_copy.wait_recv()
    out_ref[...] = (mine + sig_in[0:4, :]) * jnp.concatenate(column, axis=0)

    for copy in v_copies + v_later:
        copy.wait_send()
    for part in range(3):
        for copy in f_copies[part] + later[part]:
            copy.wait_send()
    s_copy.wait_send()


def on_device(
    vector, integrals, orbitals, alpha_addr, alpha_sign, beta_addr, beta_sign, seg_alpha, seg_beta, allowed
):
    n_aux, n_bas, _ = integrals.shape
    n_alpha = alpha_addr.shape[0]
    tall = n_aux * n_bas
    n_beta = beta_addr.shape[0]
    bf16, f32, i32 = jnp.bfloat16, jnp.float32, jnp.int32
    vmem, smem, dma = pltpu.VMEM, pltpu.SMEM, pltpu.SemaphoreType.DMA
    chips = SIDE**3
    return pl.pallas_call(
        kernel,
        out_shape=pltpu.VMEM((n_beta // (2 * chips), n_alpha), f32),
        in_specs=[pl.BlockSpec(memory_space=pltpu.HBM)] * 10,
        out_specs=pl.BlockSpec(memory_space=pltpu.VMEM),
        scratch_shapes=[
            vmem((1, n_beta), bf16),
            vmem((tall, n_bas), bf16),
            vmem((NORB, n_bas), bf16),
            vmem((ROWS, n_bas), bf16),
            vmem((n_bas, n_aux * ROWS), f32),
            vmem((tall, n_aux * ROWS), bf16),
            vmem((ROWS, tall), bf16),
            vmem((NPAIR, n_alpha), i32),
            vmem((NPAIR, n_alpha), i32),
            vmem((TALL, n_alpha), i32),
            vmem((TALL, n_alpha), f32),
            vmem((NPAIR, LANES), i32),
            vmem((NPAIR, LANES), i32),
            vmem((8, NPAIR), i32),
            vmem((8, NPAIR), f32),
            vmem((1, n_alpha), i32),
            vmem((1, n_beta), i32),
            smem((1, n_beta), i32),
            smem((NBLK, NBLK), i32),
            vmem((NBLK, NBLK), i32),
            vmem((ROWS, ROWS), f32),
            vmem((n_alpha, n_beta), f32),
            vmem((SIDE, SIDE, SIDE, n_aux, WIDE), bf16),
            vmem((SIDE, 2, SIDE, SIDE, 4, LANES), bf16),
            vmem((n_alpha, 8, LANES), f32),
            vmem((2 * n_alpha, HALF), bf16),
            vmem((8, HALF, NPAIR), bf16),
            vmem((8 * n_alpha, NPAIR), bf16),
            vmem((chips * n_aux, WIDE), bf16),
            vmem((chips * n_aux, 8 * n_alpha), bf16),
            vmem((2, WIDE, 4 * n_alpha), f32),
            vmem((8, n_alpha), f32),
            vmem((8, n_alpha), f32),
            dma((n_aux,)),
            dma((11,)),
            dma((3, 18)),
            dma((3, 18)),
            dma((len(STEPS) + 7,)),
            dma((len(STEPS) + 7,)),
            dma,
            dma,
        ],
        compiler_params=pltpu.CompilerParams(
            collective_id=0, has_side_effects=True, vmem_limit_bytes=63 << 20
        ),
        name="sigma",
    )(
        vector, integrals.transpose(1, 0, 2).reshape(tall, n_bas), orbitals,
        alpha_addr.T, alpha_sign.T, beta_addr.T, beta_sign.T,
        seg_alpha.reshape(1, -1), seg_beta.reshape(1, -1), allowed,
    )


def solution(mesh):
    rows = P(("grp", "blk"), None)
    placed = (rows, P(("grp", "blk"), None, None)) + (P(),) * 8
    return jax.shard_map(on_device, mesh=mesh, in_specs=placed, out_specs=rows, check_vma=False)
```

```python
import jax
import jax.numpy as jnp
from jax import lax
from jax.experimental import pallas as pl
from jax.experimental.pallas import tpu as pltpu
from jax.sharding import PartitionSpec as P

MESH = pl.DeviceIdType.MESH
SIDE = 4
LANES = 128
NORB = 26
ROWS = 32
NPAIR = NORB * NORB
WIDE = 768
TALL = 680
PART = 256
NBLK = 10
HALF = 256
STEPS = sorted(
    [(a, b, c) for a in range(SIDE) for b in range(SIDE) for c in range(SIDE)
     if (a, b, c) != (0, 0, 0) and 0 in (a, b, c)],
    key=lambda step: -sum(min(k, SIDE - k) for k in step),
)
PLANES = ((1, 2, 0), (2, 0, 1), (0, 1, 2))
CHUNK = 512


def kernel(
    vec_hbm, int_hbm, orb_hbm, aaddr_hbm, asign_hbm, baddr_hbm, bsign_hbm, sega_hbm, segb_hbm, allow_hbm,
    out_ref,
    vec_v, ibuf, orb_v, orb32, orep, wtab, halves, araw, sraw, atab, stab, btab, bsgn, baddr_v, bsign_v,
    sega_v, segb_v, segb_s, allow_s, allow_v, allow_b, mask,
    fbuf, vbuf, vf32, mbuf, chosen, ptt, fmat, tmat, pmat, sig_out, sig_in,
    isem, lsem, f_send, f_recv, v_send, v_recv, s_send, s_recv,
):
    grp = lax.axis_index("grp")
    blk = lax.axis_index("blk")
    core = lax.rem(grp, 2)
    here = (lax.div(grp, 2), lax.div(blk, SIDE), lax.rem(blk, SIDE))
    x, y, z = here
    position = grp * (SIDE * SIDE) + blk
    n_aux = fbuf.shape[3]
    n_alpha = aaddr_hbm.shape[1]
    tall = int_hbm.shape[0]

    def device_at(step, other=False):
        spot = [lax.rem(at + k, SIDE) for at, k in zip(here, step)]
        return (spot[0] * 2 + (1 - core if other else core), spot[1] * SIDE + spot[2])

    sibling = (x * 2 + (1 - core), blk)

    local = [
        (orb_hbm, orb_v),
        (vec_hbm, vec_v),
        (segb_hbm, segb_v),
        (sega_hbm, sega_v),
        (allow_hbm, allow_s),
        (allow_hbm, allow_v),
        (segb_hbm, segb_s),
        (baddr_hbm.at[:, pl.ds(pl.multiple_of(x * LANES, LANES), LANES)], btab),
        (bsign_hbm.at[:, pl.ds(pl.multiple_of(x * LANES, LANES), LANES)], bsgn),
        (aaddr_hbm, araw),
        (asign_hbm, sraw),
    ]
    local = [pltpu.make_async_copy(src, dst, lsem.at[i]) for i, (src, dst) in enumerate(local)]
    chunks = [(at, min(CHUNK, tall - at)) for at in range(0, tall, CHUNK)]
    slabs = [
        pltpu.make_async_copy(int_hbm.at[pl.ds(at, size), :], ibuf.at[pl.ds(at, size), :], isem.at[i])
        for i, (at, size) in enumerate(chunks)
    ]
    local[0].start()
    for copy in slabs:
        copy.start()
    local[1].start()

    barrier = pltpu.get_barrier_semaphore()
    for step in STEPS:
        pl.semaphore_signal(barrier, inc=1, device_id=device_at(step), device_id_type=MESH)
    for k in (2, 1, 3, 0):
        pl.semaphore_signal(barrier, inc=1, device_id=device_at((k, 0, 0), True), device_id_type=MESH)

    local[0].wait()
    orb32[...] = jnp.zeros_like(orb32)
    orb32[0:NORB, :] = orb_v[...]

    def remote(place, send, recv, target):
        return pltpu.make_async_remote_copy(
            src_ref=place, dst_ref=place, send_sem=send, recv_sem=recv, device_id=target, device_id_type=MESH
        )

    v_copies = [
        remote(vbuf.at[x, core, y, z], v_send.at[n], v_recv.at[n], device_at(step))
        for n, step in enumerate(STEPS) if step[0] == 0
    ]
    v_later = [
        remote(
            vbuf.at[x, core], v_send.at[len(STEPS) + n], v_recv.at[len(STEPS) + n], device_at((k, 0, 0), other)
        )
        for n, (k, other) in enumerate(((2, False), (2, True), (1, False), (3, False), (1, True), (3, True), (0, True)))
    ]
    f_copies, later = [[], [], []], [[], [], []]
    for part, (_, _, across) in enumerate(PLANES):
        lanes = pl.ds(part * PART, PART)
        for step in STEPS:
            if step[across] == 0:
                n = len(f_copies[part])
                f_copies[part].append(
                    remote(
                        fbuf.at[x, y, z, :, lanes], f_send.at[part, n], f_recv.at[part, n], device_at(step)
                    )
                )
        plane = tuple(here[axis] if axis == across else slice(None) for axis in range(3))
        for n, k in enumerate((2, 1, 3)):
            step = tuple(k if axis == across else 0 for axis in range(3))
            later[part].append(
                remote(
                    fbuf.at[plane + (slice(None), lanes)], f_send.at[part, 15 + n], f_recv.at[part, 15 + n],
                    device_at(step),
                )
            )
    def first_half(at, size):
        halves[:, at : at + size] = lax.dot_general(
            orb32[...], ibuf[at : at + size, :], (((1,), (1,)), ((), ())), preferred_element_type=jnp.float32
        ).astype(jnp.bfloat16)

    for copy in slabs[:4]:
        copy.wait()
    for at, size in chunks[:4]:
        first_half(at, size)
    lane = lax.broadcasted_iota(jnp.int32, (1, WIDE), 1)
    first = jnp.zeros((1, WIDE), jnp.int32)
    for i in range(1, NORB + 1):
        first = first + jnp.where(lane >= i * NORB, 1, 0)
    second = lane - NORB * first
    row = lax.broadcasted_iota(jnp.int32, (ROWS, WIDE), 0)
    spread = jnp.where(row == second, 1.0, 0.0).astype(jnp.bfloat16)
    repeat = jnp.where(
        lax.broadcasted_iota(jnp.int32, (ROWS, n_aux * ROWS), 0)
        == lax.rem(lax.broadcasted_iota(jnp.int32, (ROWS, n_aux * ROWS), 1), ROWS),
        1.0, 0.0,
    ).astype(jnp.bfloat16)
    orep[...] = lax.dot_general(
        orb32[...], repeat, (((0,), (0,)), ((), ())), preferred_element_type=jnp.float32
    )
    same = lax.broadcasted_iota(jnp.int32, (n_aux, n_aux * ROWS), 0) == lax.div(
        lax.broadcasted_iota(jnp.int32, (n_aux, n_aux * ROWS), 1), ROWS
    )

    @pl.loop(0, tall // (n_aux * 20), unroll=True)
    def _(i):
        rows = [jnp.where(same, orep[pl.ds(i * 20 + k, 1), :], 0.0) for k in range(20)]
        at = pl.multiple_of(i * (n_aux * 20), n_aux * 20)
        wtab[pl.ds(at, n_aux * 20), :] = jnp.concatenate(rows, axis=0).astype(jnp.bfloat16)

    for copy in slabs[4:]:
        copy.wait()
    for at, size in chunks[4:]:
        first_half(at, size)
    total = jnp.dot(halves[...], wtab[...], preferred_element_type=jnp.float32)

    local[1].wait()
    row_f = vec_v[...].astype(jnp.float32)
    pieces = [row_f[:, i * LANES : (i + 1) * LANES] for i in range(4)]
    vbuf[x, core, y, z] = jnp.concatenate(pieces, axis=0).astype(jnp.bfloat16)

    pl.semaphore_wait(barrier, len(STEPS) + SIDE)
    for copy in v_copies:
        copy.start()
    whole = lax.dot_general(
        total.astype(jnp.bfloat16), spread, (((0,), (0,)), ((), ())), preferred_element_type=jnp.float32
    )
    whole = jnp.where((row == first)[None], whole.reshape(n_aux, ROWS, WIDE), 0.0)
    fbuf[x, y, z] = jnp.sum(whole, axis=1).astype(jnp.bfloat16)


    for together in zip(*f_copies):
        for copy in together:
            copy.start()

    for copy in local[2:]:
        copy.start()

    for copy in local[2:7]:
        copy.wait()
    n_beta = mask.shape[1]
    allow_b[...] = jnp.zeros_like(allow_b)
    allow_b[0:NBLK, 0:NBLK] = allow_v[...].astype(jnp.float32)
    block_a = lax.broadcasted_iota(jnp.int32, (ROWS, n_alpha), 0) == sega_v[...]
    block_b = lax.broadcasted_iota(jnp.int32, (ROWS, n_beta), 0) == segb_v[...]
    by_block = jnp.dot(
        allow_b[...].astype(jnp.bfloat16), jnp.where(block_b, 1.0, 0.0).astype(jnp.bfloat16),
        preferred_element_type=jnp.float32,
    ).astype(jnp.bfloat16)
    mask[...] = lax.dot_general(
        jnp.where(block_a, 1.0, 0.0).astype(jnp.bfloat16), by_block,
        (((0,), (0,)), ((), ())), preferred_element_type=jnp.float32,
    )

    local[9].wait()
    local[10].wait()
    atab[TALL - 8 : TALL, :] = jnp.zeros((8, n_alpha), jnp.int32)
    stab[TALL - 8 : TALL, :] = jnp.zeros((8, n_alpha), jnp.float32)
    atab[0:NPAIR, :] = araw[...]
    stab[0:NPAIR, :] = sraw[...].astype(jnp.float32)

    local[7].wait()
    local[8].wait()
    string = lax.broadcasted_iota(jnp.int32, (8, LANES), 0)
    twin = jnp.where(string < 4, 1 - core, core)
    wanted = twin * (4 * SIDE * SIDE) + blk * 4 + lax.rem(string, 4)
    pick = jnp.where(lax.broadcasted_iota(jnp.int32, (8, LANES), 1) == wanted, 1.0, 0.0).astype(jnp.bfloat16)

    def picked(table):
        return lax.dot_general(
            pick, table.astype(jnp.float32).astype(jnp.bfloat16),
            (((1,), (1,)), ((), ())), preferred_element_type=jnp.float32,
        )

    addr = btab[...]
    high = lax.shift_right_logical(addr, 8)
    baddr_v[...] = (picked(addr - high * 256) + 256.0 * picked(high)).astype(jnp.int32)
    bsign_v[...] = picked(bsgn[...])

    @pl.loop(0, 8)
    def _(i):
        addr = lax.rem(baddr_v[pl.ds(i, 1), :], HALF)
        place = lax.broadcasted_iota(jnp.int32, (HALF, NPAIR), 0)
        chosen[i] = jnp.where(place == addr, bsign_v[pl.ds(i, 1), :], 0.0).astype(jnp.bfloat16)
    for copy in v_copies:
        copy.wait_recv()
    for copy in v_later:
        copy.start()
    for part in range(3):
        for copy in f_copies[part]:
            copy.wait_recv()
        for copy in later[part]:
            copy.start()

    for copy in v_later:
        copy.wait_recv()
    vf32[:, 0:4, :] = vbuf[...].astype(jnp.float32).reshape(n_alpha, 4, LANES)
    for i in range(4):
        lanes = slice(i * LANES, (i + 1) * LANES)
        at, to = (i // 2) * n_alpha, (i % 2) * LANES
        mbuf[at : at + n_alpha, to : to + LANES] = (vf32[:, i, :] * mask[:, lanes]).astype(jnp.bfloat16)
    for i in range(8):
        both = jnp.dot(mbuf[...], chosen[i], preferred_element_type=jnp.float32)
        ptt[i * n_alpha : (i + 1) * n_alpha, :] = jnp.where(
            baddr_v[i : i + 1, :] >= HALF, both[n_alpha:, :], both[:n_alpha, :]
        ).astype(jnp.bfloat16)

    for part in range(3):
        for copy in later[part]:
            copy.wait_recv()
    count = fmat.shape[0]
    fmat[...] = fbuf[...].astype(jnp.float32).reshape(count, WIDE).astype(jnp.bfloat16)
    tmat[...] = lax.dot_general(
        fmat[:, 0:NPAIR], ptt[...], (((1,), (1,)), ((), ())), preferred_element_type=jnp.float32
    ).astype(jnp.bfloat16)

    def half_sigma(half):
        rows = 4 * n_alpha
        pmat[half] = lax.dot_general(
            fmat[...], tmat[:, half * rows : (half + 1) * rows],
            (((0,), (0,)), ((), ())), preferred_element_type=jnp.float32,
        )

        def add_rows(i, totals):
            at = pl.ds(pl.multiple_of(i * 8, 8), 8)
            index = atab[at, :]
            sign = stab[at, :]
            return tuple(
                total + sign * jnp.take_along_axis(
                    pmat[half, at, b * n_alpha : (b + 1) * n_alpha], index, axis=1, mode="promise_in_bounds"
                )
                for b, total in enumerate(totals)
            )

        totals = lax.fori_loop(0, TALL // 8, add_rows, (jnp.zeros((8, n_alpha), jnp.float32),) * 4, unroll=True)
        return jnp.concatenate([jnp.sum(total, axis=0, keepdims=True) for total in totals], axis=0)

    sig_out[0:4, :] = half_sigma(0)
    s_copy = pltpu.make_async_remote_copy(
        src_ref=sig_out, dst_ref=sig_in, send_sem=s_send, recv_sem=s_recv, device_id=sibling, device_id_type=MESH
    )
    s_copy.start()
    mine = half_sigma(1)
    column = []
    for b in range(4):
        seg = segb_s[0, position * 4 + b]
        kept = jnp.zeros((1, n_alpha), jnp.float32)
        for block in range(NBLK):
            kept = jnp.where(sega_v[...] == block, allow_s[block, seg].astype(jnp.float32), kept)
        column.append(kept)
    s_copy.wait_recv()
    out_ref[...] = (mine + sig_in[0:4, :]) * jnp.concatenate(column, axis=0)

    for copy in v_copies + v_later:
        copy.wait_send()
    for part in range(3):
        for copy in f_copies[part] + later[part]:
            copy.wait_send()
    s_copy.wait_send()


def on_device(
    vector, integrals, orbitals, alpha_addr, alpha_sign, beta_addr, beta_sign, seg_alpha, seg_beta, allowed
):
    n_aux, n_bas, _ = integrals.shape
    n_alpha = alpha_addr.shape[0]
    tall = n_aux * n_bas
    n_beta = beta_addr.shape[0]
    bf16, f32, i32 = jnp.bfloat16, jnp.float32, jnp.int32
    vmem, smem, dma = pltpu.VMEM, pltpu.SMEM, pltpu.SemaphoreType.DMA
    chips = SIDE**3
    return pl.pallas_call(
        kernel,
        out_shape=pltpu.VMEM((n_beta // (2 * chips), n_alpha), f32),
        in_specs=[pl.BlockSpec(memory_space=pltpu.HBM)] * 10,
        out_specs=pl.BlockSpec(memory_space=pltpu.VMEM),
        scratch_shapes=[
            vmem((1, n_beta), bf16),
            vmem((tall, n_bas), bf16),
            vmem((NORB, n_bas), bf16),
            vmem((ROWS, n_bas), bf16),
            vmem((n_bas, n_aux * ROWS), f32),
            vmem((tall, n_aux * ROWS), bf16),
            vmem((ROWS, tall), bf16),
            vmem((NPAIR, n_alpha), i32),
            vmem((NPAIR, n_alpha), i32),
            vmem((TALL, n_alpha), i32),
            vmem((TALL, n_alpha), f32),
            vmem((NPAIR, LANES), i32),
            vmem((NPAIR, LANES), i32),
            vmem((8, NPAIR), i32),
            vmem((8, NPAIR), f32),
            vmem((1, n_alpha), i32),
            vmem((1, n_beta), i32),
            smem((1, n_beta), i32),
            smem((NBLK, NBLK), i32),
            vmem((NBLK, NBLK), i32),
            vmem((ROWS, ROWS), f32),
            vmem((n_alpha, n_beta), f32),
            vmem((SIDE, SIDE, SIDE, n_aux, WIDE), bf16),
            vmem((SIDE, 2, SIDE, SIDE, 4, LANES), bf16),
            vmem((n_alpha, 8, LANES), f32),
            vmem((2 * n_alpha, HALF), bf16),
            vmem((8, HALF, NPAIR), bf16),
            vmem((8 * n_alpha, NPAIR), bf16),
            vmem((chips * n_aux, WIDE), bf16),
            vmem((chips * n_aux, 8 * n_alpha), bf16),
            vmem((2, WIDE, 4 * n_alpha), f32),
            vmem((8, n_alpha), f32),
            vmem((8, n_alpha), f32),
            dma((n_aux,)),
            dma((11,)),
            dma((3, 18)),
            dma((3, 18)),
            dma((len(STEPS) + 7,)),
            dma((len(STEPS) + 7,)),
            dma,
            dma,
        ],
        compiler_params=pltpu.CompilerParams(
            collective_id=0, has_side_effects=True, vmem_limit_bytes=63 << 20
        ),
        name="sigma",
    )(
        vector, integrals.transpose(1, 0, 2).reshape(tall, n_bas), orbitals,
        alpha_addr.T, alpha_sign.T, beta_addr.T, beta_sign.T,
        seg_alpha.reshape(1, -1), seg_beta.reshape(1, -1), allowed,
    )


def solution(mesh):
    rows = P(("grp", "blk"), None)
    placed = (rows, P(("grp", "blk"), None, None)) + (P(),) * 8
    return jax.shard_map(on_device, mesh=mesh, in_specs=placed, out_specs=rows, check_vma=False)
```

```python
import jax
import jax.numpy as jnp
from jax import lax
from jax.experimental import pallas as pl
from jax.experimental.pallas import tpu as pltpu
from jax.sharding import PartitionSpec as P

MESH = pl.DeviceIdType.MESH
SIDE = 4
LANES = 128
NORB = 26
ROWS = 32
NPAIR = NORB * NORB
WIDE = 768
TALL = 680
PART = 256
NBLK = 10
HALF = 256
STEPS = sorted(
    [(a, b, c) for a in range(SIDE) for b in range(SIDE) for c in range(SIDE)
     if (a, b, c) != (0, 0, 0) and 0 in (a, b, c)],
    key=lambda step: -sum(min(k, SIDE - k) for k in step),
)
PLANES = ((1, 2, 0), (2, 0, 1), (0, 1, 2))
CHUNK = 512


def kernel(
    vec_hbm, int_hbm, orb_hbm, aaddr_hbm, asign_hbm, baddr_hbm, bsign_hbm, sega_hbm, segb_hbm, allow_hbm,
    out_ref,
    vec_v, ibuf, orb_v, orb32, orep, wtab, halves, araw, sraw, atab, stab, btab, bsgn, baddr_v, bsign_v,
    sega_v, segb_v, segb_s, allow_s, allow_v, allow_b, mask,
    fbuf, vbuf, vf32, mbuf, chosen, ptt, fmat, tmat, pmat, sig_out, sig_in,
    isem, lsem, f_send, f_recv, v_send, v_recv, s_send, s_recv,
):
    grp = lax.axis_index("grp")
    blk = lax.axis_index("blk")
    core = lax.rem(grp, 2)
    here = (lax.div(grp, 2), lax.div(blk, SIDE), lax.rem(blk, SIDE))
    x, y, z = here
    position = grp * (SIDE * SIDE) + blk
    n_aux = fbuf.shape[3]
    n_alpha = aaddr_hbm.shape[1]
    tall = int_hbm.shape[0]

    def device_at(step, other=False):
        spot = [lax.rem(at + k, SIDE) for at, k in zip(here, step)]
        return (spot[0] * 2 + (1 - core if other else core), spot[1] * SIDE + spot[2])

    sibling = (x * 2 + (1 - core), blk)

    local = [
        (orb_hbm, orb_v),
        (vec_hbm, vec_v),
        (segb_hbm, segb_v),
        (sega_hbm, sega_v),
        (allow_hbm, allow_s),
        (allow_hbm, allow_v),
        (segb_hbm, segb_s),
        (baddr_hbm.at[:, pl.ds(pl.multiple_of(x * LANES, LANES), LANES)], btab),
        (bsign_hbm.at[:, pl.ds(pl.multiple_of(x * LANES, LANES), LANES)], bsgn),
        (aaddr_hbm, araw),
        (asign_hbm, sraw),
    ]
    local = [pltpu.make_async_copy(src, dst, lsem.at[i]) for i, (src, dst) in enumerate(local)]
    chunks = [(at, min(CHUNK, tall - at)) for at in range(0, tall, CHUNK)]
    slabs = [
        pltpu.make_async_copy(int_hbm.at[pl.ds(at, size), :], ibuf.at[pl.ds(at, size), :], isem.at[i])
        for i, (at, size) in enumerate(((0, 4 * CHUNK), (4 * CHUNK, tall - 4 * CHUNK)))
    ]
    local[0].start()
    for copy in slabs:
        copy.start()
    local[1].start()

    barrier = pltpu.get_barrier_semaphore()
    for step in STEPS:
        pl.semaphore_signal(barrier, inc=1, device_id=device_at(step), device_id_type=MESH)
    for k in (2, 1, 3, 0):
        pl.semaphore_signal(barrier, inc=1, device_id=device_at((k, 0, 0), True), device_id_type=MESH)

    local[0].wait()
    orb32[...] = jnp.zeros_like(orb32)
    orb32[0:NORB, :] = orb_v[...]

    def remote(place, send, recv, target):
        return pltpu.make_async_remote_copy(
            src_ref=place, dst_ref=place, send_sem=send, recv_sem=recv, device_id=target, device_id_type=MESH
        )

    v_copies = [
        remote(vbuf.at[x, core, y, z], v_send.at[n], v_recv.at[n], device_at(step))
        for n, step in enumerate(STEPS) if step[0] == 0
    ]
    v_later = [
        remote(
            vbuf.at[x, core], v_send.at[len(STEPS) + n], v_recv.at[len(STEPS) + n], device_at((k, 0, 0), other)
        )
        for n, (k, other) in enumerate(((2, False), (2, True), (1, False), (3, False), (1, True), (3, True), (0, True)))
    ]
    f_copies, later = [[], [], []], [[], [], []]
    for part, (_, _, across) in enumerate(PLANES):
        lanes = pl.ds(part * PART, PART)
        for step in STEPS:
            if step[across] == 0:
                n = len(f_copies[part])
                f_copies[part].append(
                    remote(
                        fbuf.at[x, y, z, :, lanes], f_send.at[part, n], f_recv.at[part, n], device_at(step)
                    )
                )
        plane = tuple(here[axis] if axis == across else slice(None) for axis in range(3))
        for n, k in enumerate((2, 1, 3)):
            step = tuple(k if axis == across else 0 for axis in range(3))
            later[part].append(
                remote(
                    fbuf.at[plane + (slice(None), lanes)], f_send.at[part, 15 + n], f_recv.at[part, 15 + n],
                    device_at(step),
                )
            )
    def first_half(at, size):
        halves[:, at : at + size] = lax.dot_general(
            orb32[...], ibuf[at : at + size, :], (((1,), (1,)), ((), ())), preferred_element_type=jnp.float32
        ).astype(jnp.bfloat16)

    slabs[0].wait()
    for at, size in chunks[:4]:
        first_half(at, size)
    lane = lax.broadcasted_iota(jnp.int32, (1, WIDE), 1)
    first = jnp.zeros((1, WIDE), jnp.int32)
    for i in range(1, NORB + 1):
        first = first + jnp.where(lane >= i * NORB, 1, 0)
    second = lane - NORB * first
    row = lax.broadcasted_iota(jnp.int32, (ROWS, WIDE), 0)
    spread = jnp.where(row == second, 1.0, 0.0).astype(jnp.bfloat16)
    repeat = jnp.where(
        lax.broadcasted_iota(jnp.int32, (ROWS, n_aux * ROWS), 0)
        == lax.rem(lax.broadcasted_iota(jnp.int32, (ROWS, n_aux * ROWS), 1), ROWS),
        1.0, 0.0,
    ).astype(jnp.bfloat16)
    orep[...] = lax.dot_general(
        orb32[...], repeat, (((0,), (0,)), ((), ())), preferred_element_type=jnp.float32
    )
    same = lax.broadcasted_iota(jnp.int32, (n_aux, n_aux * ROWS), 0) == lax.div(
        lax.broadcasted_iota(jnp.int32, (n_aux, n_aux * ROWS), 1), ROWS
    )

    @pl.loop(0, tall // (n_aux * 20), unroll=True)
    def _(i):
        rows = [jnp.where(same, orep[pl.ds(i * 20 + k, 1), :], 0.0) for k in range(20)]
        at = pl.multiple_of(i * (n_aux * 20), n_aux * 20)
        wtab[pl.ds(at, n_aux * 20), :] = jnp.concatenate(rows, axis=0).astype(jnp.bfloat16)

    slabs[1].wait()
    for at, size in chunks[4:]:
        first_half(at, size)
    local[1].wait()
    row_f = vec_v[...].astype(jnp.float32)
    pieces = [row_f[:, i * LANES : (i + 1) * LANES] for i in range(4)]
    vbuf[x, core, y, z] = jnp.concatenate(pieces, axis=0).astype(jnp.bfloat16)

    pl.semaphore_wait(barrier, len(STEPS) + SIDE)
    for copy in v_copies:
        copy.start()
    total = jnp.dot(halves[...], wtab[...], preferred_element_type=jnp.float32)

    whole = lax.dot_general(
        total.astype(jnp.bfloat16), spread, (((0,), (0,)), ((), ())), preferred_element_type=jnp.float32
    )
    whole = jnp.where((row == first)[None], whole.reshape(n_aux, ROWS, WIDE), 0.0)
    fbuf[x, y, z] = jnp.sum(whole, axis=1).astype(jnp.bfloat16)


    for together in zip(*f_copies):
        for copy in together:
            copy.start()

    for copy in local[2:]:
        copy.start()

    for copy in local[2:7]:
        copy.wait()
    n_beta = mask.shape[1]
    allow_b[...] = jnp.zeros_like(allow_b)
    allow_b[0:NBLK, 0:NBLK] = allow_v[...].astype(jnp.float32)
    block_a = lax.broadcasted_iota(jnp.int32, (ROWS, n_alpha), 0) == sega_v[...]
    block_b = lax.broadcasted_iota(jnp.int32, (ROWS, n_beta), 0) == segb_v[...]
    by_block = jnp.dot(
        allow_b[...].astype(jnp.bfloat16), jnp.where(block_b, 1.0, 0.0).astype(jnp.bfloat16),
        preferred_element_type=jnp.float32,
    ).astype(jnp.bfloat16)
    mask[...] = lax.dot_general(
        jnp.where(block_a, 1.0, 0.0).astype(jnp.bfloat16), by_block,
        (((0,), (0,)), ((), ())), preferred_element_type=jnp.float32,
    )

    local[9].wait()
    local[10].wait()
    atab[TALL - 8 : TALL, :] = jnp.zeros((8, n_alpha), jnp.int32)
    stab[TALL - 8 : TALL, :] = jnp.zeros((8, n_alpha), jnp.float32)
    atab[0:NPAIR, :] = araw[...]
    stab[0:NPAIR, :] = sraw[...].astype(jnp.float32)

    local[7].wait()
    local[8].wait()
    string = lax.broadcasted_iota(jnp.int32, (8, LANES), 0)
    twin = jnp.where(string < 4, 1 - core, core)
    wanted = twin * (4 * SIDE * SIDE) + blk * 4 + lax.rem(string, 4)
    pick = jnp.where(lax.broadcasted_iota(jnp.int32, (8, LANES), 1) == wanted, 1.0, 0.0).astype(jnp.bfloat16)

    def picked(table):
        return lax.dot_general(
            pick, table.astype(jnp.float32).astype(jnp.bfloat16),
            (((1,), (1,)), ((), ())), preferred_element_type=jnp.float32,
        )

    addr = btab[...]
    high = lax.shift_right_logical(addr, 8)
    baddr_v[...] = (picked(addr - high * 256) + 256.0 * picked(high)).astype(jnp.int32)
    bsign_v[...] = picked(bsgn[...])

    @pl.loop(0, 8)
    def _(i):
        addr = lax.rem(baddr_v[pl.ds(i, 1), :], HALF)
        place = lax.broadcasted_iota(jnp.int32, (HALF, NPAIR), 0)
        chosen[i] = jnp.where(place == addr, bsign_v[pl.ds(i, 1), :], 0.0).astype(jnp.bfloat16)
    for copy in v_copies:
        copy.wait_recv()
    for copy in v_later:
        copy.start()
    for part in range(3):
        for copy in f_copies[part]:
            copy.wait_recv()
        for copy in later[part]:
            copy.start()

    for copy in v_later:
        copy.wait_recv()
    vf32[:, 0:4, :] = vbuf[...].astype(jnp.float32).reshape(n_alpha, 4, LANES)
    for i in range(4):
        lanes = slice(i * LANES, (i + 1) * LANES)
        at, to = (i // 2) * n_alpha, (i % 2) * LANES
        mbuf[at : at + n_alpha, to : to + LANES] = (vf32[:, i, :] * mask[:, lanes]).astype(jnp.bfloat16)
    for i in range(8):
        both = jnp.dot(mbuf[...], chosen[i], preferred_element_type=jnp.float32)
        ptt[i * n_alpha : (i + 1) * n_alpha, :] = jnp.where(
            baddr_v[i : i + 1, :] >= HALF, both[n_alpha:, :], both[:n_alpha, :]
        ).astype(jnp.bfloat16)

    for part in range(3):
        for copy in later[part]:
            copy.wait_recv()
    count = fmat.shape[0]
    fmat[...] = fbuf[...].astype(jnp.float32).reshape(count, WIDE).astype(jnp.bfloat16)
    tmat[...] = lax.dot_general(
        fmat[:, 0:NPAIR], ptt[...], (((1,), (1,)), ((), ())), preferred_element_type=jnp.float32
    ).astype(jnp.bfloat16)

    def half_sigma(half):
        rows = 4 * n_alpha
        pmat[half] = lax.dot_general(
            fmat[...], tmat[:, half * rows : (half + 1) * rows],
            (((0,), (0,)), ((), ())), preferred_element_type=jnp.float32,
        )

        def add_rows(i, totals):
            at = pl.ds(pl.multiple_of(i * 8, 8), 8)
            index = atab[at, :]
            sign = stab[at, :]
            return tuple(
                total + sign * jnp.take_along_axis(
                    pmat[half, at, b * n_alpha : (b + 1) * n_alpha], index, axis=1, mode="promise_in_bounds"
                )
                for b, total in enumerate(totals)
            )

        totals = lax.fori_loop(0, TALL // 8, add_rows, (jnp.zeros((8, n_alpha), jnp.float32),) * 4, unroll=True)
        return jnp.concatenate([jnp.sum(total, axis=0, keepdims=True) for total in totals], axis=0)

    sig_out[0:4, :] = half_sigma(0)
    s_copy = pltpu.make_async_remote_copy(
        src_ref=sig_out, dst_ref=sig_in, send_sem=s_send, recv_sem=s_recv, device_id=sibling, device_id_type=MESH
    )
    s_copy.start()
    mine = half_sigma(1)
    column = []
    for b in range(4):
        seg = segb_s[0, position * 4 + b]
        kept = jnp.zeros((1, n_alpha), jnp.float32)
        for block in range(NBLK):
            kept = jnp.where(sega_v[...] == block, allow_s[block, seg].astype(jnp.float32), kept)
        column.append(kept)
    s_copy.wait_recv()
    out_ref[...] = (mine + sig_in[0:4, :]) * jnp.concatenate(column, axis=0)

    for copy in v_copies + v_later:
        copy.wait_send()
    for part in range(3):
        for copy in f_copies[part] + later[part]:
            copy.wait_send()
    s_copy.wait_send()


def on_device(
    vector, integrals, orbitals, alpha_addr, alpha_sign, beta_addr, beta_sign, seg_alpha, seg_beta, allowed
):
    n_aux, n_bas, _ = integrals.shape
    n_alpha = alpha_addr.shape[0]
    tall = n_aux * n_bas
    n_beta = beta_addr.shape[0]
    bf16, f32, i32 = jnp.bfloat16, jnp.float32, jnp.int32
    vmem, smem, dma = pltpu.VMEM, pltpu.SMEM, pltpu.SemaphoreType.DMA
    chips = SIDE**3
    return pl.pallas_call(
        kernel,
        out_shape=pltpu.VMEM((n_beta // (2 * chips), n_alpha), f32),
        in_specs=[pl.BlockSpec(memory_space=pltpu.HBM)] * 10,
        out_specs=pl.BlockSpec(memory_space=pltpu.VMEM),
        scratch_shapes=[
            vmem((1, n_beta), bf16),
            vmem((tall, n_bas), bf16),
            vmem((NORB, n_bas), bf16),
            vmem((ROWS, n_bas), bf16),
            vmem((n_bas, n_aux * ROWS), f32),
            vmem((tall, n_aux * ROWS), bf16),
            vmem((ROWS, tall), bf16),
            vmem((NPAIR, n_alpha), i32),
            vmem((NPAIR, n_alpha), i32),
            vmem((TALL, n_alpha), i32),
            vmem((TALL, n_alpha), f32),
            vmem((NPAIR, LANES), i32),
            vmem((NPAIR, LANES), i32),
            vmem((8, NPAIR), i32),
            vmem((8, NPAIR), f32),
            vmem((1, n_alpha), i32),
            vmem((1, n_beta), i32),
            smem((1, n_beta), i32),
            smem((NBLK, NBLK), i32),
            vmem((NBLK, NBLK), i32),
            vmem((ROWS, ROWS), f32),
            vmem((n_alpha, n_beta), f32),
            vmem((SIDE, SIDE, SIDE, n_aux, WIDE), bf16),
            vmem((SIDE, 2, SIDE, SIDE, 4, LANES), bf16),
            vmem((n_alpha, 8, LANES), f32),
            vmem((2 * n_alpha, HALF), bf16),
            vmem((8, HALF, NPAIR), bf16),
            vmem((8 * n_alpha, NPAIR), bf16),
            vmem((chips * n_aux, WIDE), bf16),
            vmem((chips * n_aux, 8 * n_alpha), bf16),
            vmem((2, WIDE, 4 * n_alpha), f32),
            vmem((8, n_alpha), f32),
            vmem((8, n_alpha), f32),
            dma((n_aux,)),
            dma((11,)),
            dma((3, 18)),
            dma((3, 18)),
            dma((len(STEPS) + 7,)),
            dma((len(STEPS) + 7,)),
            dma,
            dma,
        ],
        compiler_params=pltpu.CompilerParams(
            collective_id=0, has_side_effects=True, vmem_limit_bytes=63 << 20
        ),
        name="sigma",
    )(
        vector, integrals.transpose(1, 0, 2).reshape(tall, n_bas), orbitals,
        alpha_addr.T, alpha_sign.T, beta_addr.T, beta_sign.T,
        seg_alpha.reshape(1, -1), seg_beta.reshape(1, -1), allowed,
    )


def solution(mesh):
    rows = P(("grp", "blk"), None)
    placed = (rows, P(("grp", "blk"), None, None)) + (P(),) * 8
    return jax.shard_map(on_device, mesh=mesh, in_specs=placed, out_specs=rows, check_vma=False)
```

```python
import jax
import jax.numpy as jnp
from jax import lax
from jax.experimental import pallas as pl
from jax.experimental.pallas import tpu as pltpu
from jax.sharding import PartitionSpec as P

MESH = pl.DeviceIdType.MESH
SIDE = 4
LANES = 128
NORB = 26
ROWS = 32
NPAIR = NORB * NORB
WIDE = 768
TALL = 680
PART = 256
NBLK = 10
HALF = 256
STEPS = sorted(
    [(a, b, c) for a in range(SIDE) for b in range(SIDE) for c in range(SIDE)
     if (a, b, c) != (0, 0, 0) and 0 in (a, b, c)],
    key=lambda step: -sum(min(k, SIDE - k) for k in step),
)
PLANES = ((1, 2, 0), (2, 0, 1), (0, 1, 2))
CHUNK = 512


def kernel(
    vec_hbm, int_hbm, orb_hbm, aaddr_hbm, asign_hbm, baddr_hbm, bsign_hbm, sega_hbm, segb_hbm, allow_hbm,
    out_ref,
    vec_v, ibuf, orb_v, orb32, orep, wtab, halves, araw, sraw, atab, stab, btab, bsgn, baddr_v, bsign_v,
    sega_v, segb_v, segb_s, allow_s, allow_v, allow_b, mask,
    fbuf, vbuf, vf32, mbuf, chosen, ptt, fmat, tmat, pmat, sig_out, sig_in,
    isem, lsem, f_send, f_recv, v_send, v_recv, s_send, s_recv,
):
    grp = lax.axis_index("grp")
    blk = lax.axis_index("blk")
    core = lax.rem(grp, 2)
    here = (lax.div(grp, 2), lax.div(blk, SIDE), lax.rem(blk, SIDE))
    x, y, z = here
    position = grp * (SIDE * SIDE) + blk
    n_aux = fbuf.shape[3]
    n_alpha = aaddr_hbm.shape[1]
    tall = int_hbm.shape[0]

    def device_at(step, other=False):
        spot = [lax.rem(at + k, SIDE) for at, k in zip(here, step)]
        return (spot[0] * 2 + (1 - core if other else core), spot[1] * SIDE + spot[2])

    sibling = (x * 2 + (1 - core), blk)

    local = [
        (orb_hbm, orb_v),
        (vec_hbm, vec_v),
        (segb_hbm, segb_v),
        (sega_hbm, sega_v),
        (allow_hbm, allow_s),
        (allow_hbm, allow_v),
        (segb_hbm, segb_s),
        (baddr_hbm.at[:, pl.ds(pl.multiple_of(x * LANES, LANES), LANES)], btab),
        (bsign_hbm.at[:, pl.ds(pl.multiple_of(x * LANES, LANES), LANES)], bsgn),
        (aaddr_hbm, araw),
        (asign_hbm, sraw),
    ]
    local = [pltpu.make_async_copy(src, dst, lsem.at[i]) for i, (src, dst) in enumerate(local)]
    chunks = [(at, min(CHUNK, tall - at)) for at in range(0, tall, CHUNK)]
    slabs = [
        pltpu.make_async_copy(int_hbm.at[pl.ds(at, size), :], ibuf.at[pl.ds(at, size), :], isem.at[i])
        for i, (at, size) in enumerate(chunks)
    ]
    local[0].start()
    for copy in slabs:
        copy.start()
    local[1].start()

    barrier = pltpu.get_barrier_semaphore()
    for step in STEPS:
        pl.semaphore_signal(barrier, inc=1, device_id=device_at(step), device_id_type=MESH)
    for k in (2, 1, 3, 0):
        pl.semaphore_signal(barrier, inc=1, device_id=device_at((k, 0, 0), True), device_id_type=MESH)

    local[0].wait()
    orb32[...] = jnp.zeros_like(orb32)
    orb32[0:NORB, :] = orb_v[...]

    def remote(place, send, recv, target):
        return pltpu.make_async_remote_copy(
            src_ref=place, dst_ref=place, send_sem=send, recv_sem=recv, device_id=target, device_id_type=MESH
        )

    v_copies = [
        remote(vbuf.at[x, core, y, z], v_send.at[n], v_recv.at[n], device_at(step))
        for n, step in enumerate(STEPS) if step[0] == 0
    ]
    v_later = [
        remote(
            vbuf.at[x, core], v_send.at[len(STEPS) + n], v_recv.at[len(STEPS) + n], device_at((k, 0, 0), other)
        )
        for n, (k, other) in enumerate(((2, False), (2, True), (1, False), (3, False), (1, True), (3, True), (0, True)))
    ]
    f_copies, later = [[], [], []], [[], [], []]
    for part, (_, _, across) in enumerate(PLANES):
        lanes = pl.ds(part * PART, PART)
        for step in STEPS:
            if step[across] == 0:
                n = len(f_copies[part])
                f_copies[part].append(
                    remote(
                        fbuf.at[x, y, z, :, lanes], f_send.at[part, n], f_recv.at[part, n], device_at(step)
                    )
                )
        plane = tuple(here[axis] if axis == across else slice(None) for axis in range(3))
        for n, k in enumerate((2, 1, 3)):
            step = tuple(k if axis == across else 0 for axis in range(3))
            later[part].append(
                remote(
                    fbuf.at[plane + (slice(None), lanes)], f_send.at[part, 15 + n], f_recv.at[part, 15 + n],
                    device_at(step),
                )
            )
    def first_half(at, size):
        halves[:, at : at + size] = lax.dot_general(
            orb32[...], ibuf[at : at + size, :], (((1,), (1,)), ((), ())), preferred_element_type=jnp.float32
        ).astype(jnp.bfloat16)

    for copy in slabs[:4]:
        copy.wait()
    for at, size in chunks[:4]:
        first_half(at, size)
    lane = lax.broadcasted_iota(jnp.int32, (1, WIDE), 1)
    first = jnp.zeros((1, WIDE), jnp.int32)
    for i in range(1, NORB + 1):
        first = first + jnp.where(lane >= i * NORB, 1, 0)
    second = lane - NORB * first
    row = lax.broadcasted_iota(jnp.int32, (ROWS, WIDE), 0)
    spread = jnp.where(row == second, 1.0, 0.0).astype(jnp.bfloat16)
    repeat = jnp.where(
        lax.broadcasted_iota(jnp.int32, (ROWS, n_aux * ROWS), 0)
        == lax.rem(lax.broadcasted_iota(jnp.int32, (ROWS, n_aux * ROWS), 1), ROWS),
        1.0, 0.0,
    ).astype(jnp.bfloat16)
    orep[...] = lax.dot_general(
        orb32[...], repeat, (((0,), (0,)), ((), ())), preferred_element_type=jnp.float32
    )
    same = lax.broadcasted_iota(jnp.int32, (n_aux, n_aux * ROWS), 0) == lax.div(
        lax.broadcasted_iota(jnp.int32, (n_aux, n_aux * ROWS), 1), ROWS
    )

    @pl.loop(0, tall // (n_aux * 20), unroll=True)
    def _(i):
        rows = [jnp.where(same, orep[pl.ds(i * 20 + k, 1), :], 0.0) for k in range(20)]
        at = pl.multiple_of(i * (n_aux * 20), n_aux * 20)
        wtab[pl.ds(at, n_aux * 20), :] = jnp.concatenate(rows, axis=0).astype(jnp.bfloat16)

    for copy in slabs[4:]:
        copy.wait()
    for at, size in chunks[4:]:
        first_half(at, size)
    total = jnp.dot(halves[...], wtab[...], preferred_element_type=jnp.float32)

    local[1].wait()
    row_f = vec_v[...].astype(jnp.float32)
    pieces = [row_f[:, i * LANES : (i + 1) * LANES] for i in range(4)]
    vbuf[x, core, y, z] = jnp.concatenate(pieces, axis=0).astype(jnp.bfloat16)

    pl.semaphore_wait(barrier, len(STEPS) + SIDE)
    for copy in v_copies:
        copy.start()
    whole = lax.dot_general(
        total.astype(jnp.bfloat16), spread, (((0,), (0,)), ((), ())), preferred_element_type=jnp.float32
    )
    whole = jnp.where((row == first)[None], whole.reshape(n_aux, ROWS, WIDE), 0.0)
    fbuf[x, y, z] = jnp.sum(whole, axis=1).astype(jnp.bfloat16)


    for together in zip(*f_copies):
        for copy in together:
            copy.start()

    for copy in local[2:]:
        copy.start()

    for copy in local[2:7]:
        copy.wait()
    n_beta = mask.shape[1]
    allow_b[...] = jnp.zeros_like(allow_b)
    allow_b[0:NBLK, 0:NBLK] = allow_v[...].astype(jnp.float32)
    block_a = lax.broadcasted_iota(jnp.int32, (ROWS, n_alpha), 0) == sega_v[...]
    block_b = lax.broadcasted_iota(jnp.int32, (ROWS, n_beta), 0) == segb_v[...]
    by_block = jnp.dot(
        allow_b[...].astype(jnp.bfloat16), jnp.where(block_b, 1.0, 0.0).astype(jnp.bfloat16),
        preferred_element_type=jnp.float32,
    ).astype(jnp.bfloat16)
    mask[...] = lax.dot_general(
        jnp.where(block_a, 1.0, 0.0).astype(jnp.bfloat16), by_block,
        (((0,), (0,)), ((), ())), preferred_element_type=jnp.float32,
    )

    local[9].wait()
    local[10].wait()
    atab[TALL - 8 : TALL, :] = jnp.zeros((8, n_alpha), jnp.int32)
    stab[TALL - 8 : TALL, :] = jnp.zeros((8, n_alpha), jnp.float32)
    atab[0:NPAIR, :] = araw[...]
    stab[0:NPAIR, :] = sraw[...].astype(jnp.float32)

    local[7].wait()
    local[8].wait()
    string = lax.broadcasted_iota(jnp.int32, (8, LANES), 0)
    twin = jnp.where(string < 4, 1 - core, core)
    wanted = twin * (4 * SIDE * SIDE) + blk * 4 + lax.rem(string, 4)
    pick = jnp.where(lax.broadcasted_iota(jnp.int32, (8, LANES), 1) == wanted, 1.0, 0.0).astype(jnp.bfloat16)

    def picked(table):
        return lax.dot_general(
            pick, table.astype(jnp.float32).astype(jnp.bfloat16),
            (((1,), (1,)), ((), ())), preferred_element_type=jnp.float32,
        )

    addr = btab[...]
    high = lax.shift_right_logical(addr, 8)
    baddr_v[...] = (picked(addr - high * 256) + 256.0 * picked(high)).astype(jnp.int32)
    bsign_v[...] = picked(bsgn[...])

    @pl.loop(0, 8)
    def _(i):
        addr = lax.rem(baddr_v[pl.ds(i, 1), :], HALF)
        place = lax.broadcasted_iota(jnp.int32, (HALF, NPAIR), 0)
        chosen[i] = jnp.where(place == addr, bsign_v[pl.ds(i, 1), :], 0.0).astype(jnp.bfloat16)
    for copy in v_copies:
        copy.wait_recv()
    for copy in v_later:
        copy.start()
    for part in range(3):
        for copy in f_copies[part]:
            copy.wait_recv()
        for copy in later[part]:
            copy.start()

    for copy in v_later:
        copy.wait_recv()
    vf32[:, 0:4, :] = vbuf[...].astype(jnp.float32).reshape(n_alpha, 4, LANES)
    for i in range(4):
        lanes = slice(i * LANES, (i + 1) * LANES)
        at, to = (i // 2) * n_alpha, (i % 2) * LANES
        mbuf[at : at + n_alpha, to : to + LANES] = (vf32[:, i, :] * mask[:, lanes]).astype(jnp.bfloat16)
    for i in range(8):
        both = jnp.dot(mbuf[...], chosen[i], preferred_element_type=jnp.float32)
        ptt[i * n_alpha : (i + 1) * n_alpha, :] = jnp.where(
            baddr_v[i : i + 1, :] >= HALF, both[n_alpha:, :], both[:n_alpha, :]
        ).astype(jnp.bfloat16)

    for copy in v_copies + v_later:
        copy.wait_send()
    for part in range(3):
        for copy in f_copies[part]:
            copy.wait_send()
    for part in range(3):
        for copy in later[part]:
            copy.wait_recv()
    count = fmat.shape[0]
    fmat[...] = fbuf[...].astype(jnp.float32).reshape(count, WIDE).astype(jnp.bfloat16)
    tmat[...] = lax.dot_general(
        fmat[:, 0:NPAIR], ptt[...], (((1,), (1,)), ((), ())), preferred_element_type=jnp.float32
    ).astype(jnp.bfloat16)

    def half_sigma(half):
        rows = 4 * n_alpha
        pmat[half] = lax.dot_general(
            fmat[...], tmat[:, half * rows : (half + 1) * rows],
            (((0,), (0,)), ((), ())), preferred_element_type=jnp.float32,
        )

        def add_rows(i, totals):
            at = pl.ds(pl.multiple_of(i * 8, 8), 8)
            index = atab[at, :]
            sign = stab[at, :]
            return tuple(
                total + sign * jnp.take_along_axis(
                    pmat[half, at, b * n_alpha : (b + 1) * n_alpha], index, axis=1, mode="promise_in_bounds"
                )
                for b, total in enumerate(totals)
            )

        totals = lax.fori_loop(0, TALL // 8, add_rows, (jnp.zeros((8, n_alpha), jnp.float32),) * 4, unroll=True)
        return jnp.concatenate([jnp.sum(total, axis=0, keepdims=True) for total in totals], axis=0)

    sig_out[0:4, :] = half_sigma(0)
    s_copy = pltpu.make_async_remote_copy(
        src_ref=sig_out, dst_ref=sig_in, send_sem=s_send, recv_sem=s_recv, device_id=sibling, device_id_type=MESH
    )
    s_copy.start()
    mine = half_sigma(1)
    column = []
    for b in range(4):
        seg = segb_s[0, position * 4 + b]
        kept = jnp.zeros((1, n_alpha), jnp.float32)
        for block in range(NBLK):
            kept = jnp.where(sega_v[...] == block, allow_s[block, seg].astype(jnp.float32), kept)
        column.append(kept)
    s_copy.wait_recv()
    out_ref[...] = (mine + sig_in[0:4, :]) * jnp.concatenate(column, axis=0)

    for part in range(3):
        for copy in later[part]:
            copy.wait_send()
    s_copy.wait_send()


def on_device(
    vector, integrals, orbitals, alpha_addr, alpha_sign, beta_addr, beta_sign, seg_alpha, seg_beta, allowed
):
    n_aux, n_bas, _ = integrals.shape
    n_alpha = alpha_addr.shape[0]
    tall = n_aux * n_bas
    n_beta = beta_addr.shape[0]
    bf16, f32, i32 = jnp.bfloat16, jnp.float32, jnp.int32
    vmem, smem, dma = pltpu.VMEM, pltpu.SMEM, pltpu.SemaphoreType.DMA
    chips = SIDE**3
    return pl.pallas_call(
        kernel,
        out_shape=pltpu.VMEM((n_beta // (2 * chips), n_alpha), f32),
        in_specs=[pl.BlockSpec(memory_space=pltpu.HBM)] * 10,
        out_specs=pl.BlockSpec(memory_space=pltpu.VMEM),
        scratch_shapes=[
            vmem((1, n_beta), bf16),
            vmem((tall, n_bas), bf16),
            vmem((NORB, n_bas), bf16),
            vmem((ROWS, n_bas), bf16),
            vmem((n_bas, n_aux * ROWS), f32),
            vmem((tall, n_aux * ROWS), bf16),
            vmem((ROWS, tall), bf16),
            vmem((NPAIR, n_alpha), i32),
            vmem((NPAIR, n_alpha), i32),
            vmem((TALL, n_alpha), i32),
            vmem((TALL, n_alpha), f32),
            vmem((NPAIR, LANES), i32),
            vmem((NPAIR, LANES), i32),
            vmem((8, NPAIR), i32),
            vmem((8, NPAIR), f32),
            vmem((1, n_alpha), i32),
            vmem((1, n_beta), i32),
            smem((1, n_beta), i32),
            smem((NBLK, NBLK), i32),
            vmem((NBLK, NBLK), i32),
            vmem((ROWS, ROWS), f32),
            vmem((n_alpha, n_beta), f32),
            vmem((SIDE, SIDE, SIDE, n_aux, WIDE), bf16),
            vmem((SIDE, 2, SIDE, SIDE, 4, LANES), bf16),
            vmem((n_alpha, 8, LANES), f32),
            vmem((2 * n_alpha, HALF), bf16),
            vmem((8, HALF, NPAIR), bf16),
            vmem((8 * n_alpha, NPAIR), bf16),
            vmem((chips * n_aux, WIDE), bf16),
            vmem((chips * n_aux, 8 * n_alpha), bf16),
            vmem((2, WIDE, 4 * n_alpha), f32),
            vmem((8, n_alpha), f32),
            vmem((8, n_alpha), f32),
            dma((n_aux,)),
            dma((11,)),
            dma((3, 18)),
            dma((3, 18)),
            dma((len(STEPS) + 7,)),
            dma((len(STEPS) + 7,)),
            dma,
            dma,
        ],
        compiler_params=pltpu.CompilerParams(
            collective_id=0, has_side_effects=True, vmem_limit_bytes=63 << 20
        ),
        name="sigma",
    )(
        vector, integrals.transpose(1, 0, 2).reshape(tall, n_bas), orbitals,
        alpha_addr.T, alpha_sign.T, beta_addr.T, beta_sign.T,
        seg_alpha.reshape(1, -1), seg_beta.reshape(1, -1), allowed,
    )


def solution(mesh):
    rows = P(("grp", "blk"), None)
    placed = (rows, P(("grp", "blk"), None, None)) + (P(),) * 8
    return jax.shard_map(on_device, mesh=mesh, in_specs=placed, out_specs=rows, check_vma=False)
```
